32 devices in a mesh: ens: 2 (over core), gy: 4 (over y, x), gz: 4 (over z).
Axes of the slice: x: 2, y: 2, z: 4, core: 2. Of those that a mesh axis runs over, the one named last changes fastest.
Arguments:
- state: float32 [2, 4, 16, 64, 512], P('ens', None, None, 'gy', 'gz'), parts along dimension 0, may hold values from -32 to 32
- member_set: int32 [2], P('ens'), parts along dimension 0, may hold values from 0 to 15
- courant_table: float32 [16, 3], replicated, may hold values from -0.3 to 0.3
- diffusion_table: float32 [16, 4], replicated, may hold values from 0.05 to 1
- reaction_table: float32 [16, 4, 4], replicated, may hold values from -3 to 3
- quadratic_table: float32 [16, 4], replicated, may hold values from -1 to 1
Outputs:
- state_out: float32 [2, 4, 16, 64, 512], P('ens', None, None, 'gy', 'gz'), parts along dimension 0
The draws below stay inside these ranges and needn't reach their ends.
There are 2 independent parts, one for each index of `ens`. The reference program is written for one: setup_inputs(seed, part) draws one part's arguments, and reference() takes and returns one part's arrays. A program takes and returns all parts, laid end to end along the dimension named above; an argument that names none is the same for every part. Nothing has to cross between parts.
All inputs are finite; a program needn't handle non-finite values.
Results may differ from the reference program's by a relative error of at most 0.00024.
Values sent between devices are 32-bit elements; how exact they have to be, the bound alone decides.
A program may use at most 64 MiB of HBM per device.

```python
import math
import jax
import jax.numpy as jnp
from jax import lax

SPECIES = 4
SETS = 16
ITERS = 4
MEMBERS = 1
NX = 16
NY = 64
NZ = 512


def draw_state(key, part):
    noise_key, y_key, z_key = jax.random.split(key, 3)
    dims_all = (MEMBERS, SPECIES, NX, NY, NZ)
    rising = jnp.arange(NZ, dtype=jnp.float32) / NZ
    jitter_y = jax.random.uniform(y_key, (NY,), minval=0.0, maxval=1.0)
    jitter_z = jax.random.uniform(z_key, (NZ,), minval=0.0, maxval=1.0)
    log_scale = math.log(3.0) * rising[None, :] + 0.5 * math.log(10.0) * (jitter_y[:, None] + jitter_z[None, :] - 1.0)
    magnitude = jnp.exp(log_scale)
    baseline = jax.random.normal(noise_key, dims_all)
    return jnp.clip(baseline * magnitude[None, None, None, :, :], -32.0, 32.0).astype(jnp.float32)


def gaussian(stream_key, dims, width, limit, kind=jnp.bfloat16):
    result = jax.random.normal(stream_key, dims, jnp.float32) * width
    return jnp.minimum(jnp.maximum(result, -limit), limit).astype(kind)


def setup_inputs(seed: int = 0, part: int = 0) -> dict:
    seeds = jax.random.split(jax.random.key(seed), 7)
    part_keys = jax.random.split(jax.random.fold_in(seeds[6], part), 7)
    return {
        "state": draw_state(jax.random.fold_in(jax.random.fold_in(seeds[6], part), 71), part),
        "member_set": jax.random.randint(part_keys[1], (MEMBERS,), 0, SETS).astype(jnp.int32),
        "courant_table": jnp.clip(jax.random.uniform(seeds[2], (SETS, 3), jnp.float32, -0.3, 0.3), -0.3, 0.3),
        "diffusion_table": jnp.clip(jnp.exp(jax.random.uniform(seeds[3], (SETS, SPECIES), jnp.float32, math.log(0.05), math.log(1.0))), 0.05, 1.0),
        "reaction_table": gaussian(seeds[4], (SETS, SPECIES, SPECIES), 0.3, 3.0, jnp.float32),
        "quadratic_table": jnp.clip(jax.random.uniform(seeds[5], (SETS, SPECIES), jnp.float32, -1.0, 1.0), -1.0, 1.0),
    }


def lookup(member_set, coeff_table):
    onehot = (member_set[:, None] == jnp.arange(coeff_table.shape[0], dtype=jnp.int32)[None, :]).astype(coeff_table.dtype)
    flattened = coeff_table.reshape(coeff_table.shape[0], -1)
    picked = lax.optimization_barrier(jnp.sum(onehot[:, :, None] * flattened[None, :, :], axis=1))
    return picked.reshape((member_set.shape[0],) + coeff_table.shape[1:])

def spread_out(values):
    return values[:, None, None, None, None]

def beside_all(padded, spatial, offset):
    slicer = [slice(None), slice(None), slice(1, -1), slice(1, -1), slice(1, -1)]
    slicer[spatial] = slice(offset, padded.shape[spatial] - 2 + offset)
    return padded[tuple(slicer)]

def explicit_section(padded, current, courant, reaction, quadratic):
    running = current
    for spatial in range(3):
        velocity = spread_out(courant[:, spatial])
        behind = beside_all(padded, spatial + 2, 0)
        beyond = beside_all(padded, spatial + 2, 2)
        running = running - jnp.maximum(velocity, 0.0) * (current - behind) - jnp.minimum(velocity, 0.0) * (beyond - current)
    linear = jnp.einsum('mkl,mlxyz->mkxyz', reaction, current, precision=lax.Precision.HIGHEST)
    leading = current[:, 0]
    partner = current[:, 1]
    coupled = leading * partner / (1.0 + leading * leading + partner * partner)
    return running + linear + quadratic[:, :, None, None, None] * coupled[:, None]

def implicit_apply(padded, current, diffuse):
    beside = beside_all(padded, 2, 0) + beside_all(padded, 2, 2)
    beside = beside + beside_all(padded, 3, 0) + beside_all(padded, 3, 2)
    beside = beside + beside_all(padded, 4, 0) + beside_all(padded, 4, 2)
    strength = diffuse[:, :, None, None, None]
    return (1.0 + 6.0 * strength) * current - strength * beside

def inner_product(left_side, right_side):
    return lax.optimization_barrier(jnp.sum(left_side * right_side, axis=(1, 2, 3, 4)))

def least_squares(hessen, beta, iters):
    target = [beta] + [jnp.zeros_like(beta)] * iters
    cosines = []
    sine_list = []
    triangle = []
    for column in range(iters):
        entries = list(hessen[column])
        for earlier in range(column):
            rotated = cosines[earlier] * entries[earlier] + sine_list[earlier] * entries[earlier + 1]
            entries[earlier + 1] = -sine_list[earlier] * entries[earlier] + cosines[earlier] * entries[earlier + 1]
            entries[earlier] = rotated
        radius = jnp.sqrt(entries[column] * entries[column] + entries[column + 1] * entries[column + 1])
        cosine = entries[column] / radius
        sine_val = entries[column + 1] / radius
        entries[column] = radius
        target[column + 1] = -sine_val * target[column]
        target[column] = cosine * target[column]
        cosines.append(cosine)
        sine_list.append(sine_val)
        triangle.append(entries[:column + 1])
    coeffs = [None] * iters
    for column in reversed(range(iters)):
        running = target[column]
        for further in range(column + 1, iters):
            running = running - triangle[further][column] * coeffs[further]
        coeffs[column] = running / triangle[column][column]
    return coeffs

def full_pad(current):
    return jnp.pad(current, ((0, 0), (0, 0), (1, 1), (1, 1), (1, 1)))

def reference(state, member_set, courant_table, diffusion_table, reaction_table, quadratic_table):
    courant = lookup(member_set, courant_table)
    diffuse = lookup(member_set, diffusion_table)
    reaction = lookup(member_set, reaction_table)
    quadratic = lookup(member_set, quadratic_table)
    source = explicit_section(full_pad(state), state, courant, reaction, quadratic)
    beta = jnp.sqrt(inner_product(source, source))
    basis = [source * spread_out(1.0 / beta)]
    hessen = []
    for column in range(ITERS):
        image = implicit_apply(full_pad(basis[column]), basis[column], diffuse)
        projections = [inner_product(basis[earlier], image) for earlier in range(column + 1)]
        remainder = image
        for earlier in range(column + 1):
            remainder = remainder - spread_out(projections[earlier]) * basis[earlier]
        norm_next = jnp.sqrt(inner_product(remainder, remainder))
        hessen.append(projections + [norm_next])
        if column + 1 < ITERS:
            basis.append(remainder * spread_out(1.0 / norm_next))
    coeffs = least_squares(hessen, beta, ITERS)
    state_out = spread_out(coeffs[0]) * basis[0]
    for column in range(1, ITERS):
        state_out = state_out + spread_out(coeffs[column]) * basis[column]
    return state_out
```

```python
import functools

import jax
import jax.numpy as jnp
from jax import lax
from jax.experimental import pallas as pl
from jax.experimental.pallas import tpu as pltpu
from jax.sharding import PartitionSpec as P

ITERS = 4
TOP = 8


def kernel(
    ny, nz,
    state_ref, set_ref, courant_ref, diffuse_ref, react_ref, quad_ref,
    out_ref,
    cells, padded, image, basis,
    ysend, yrecv, zsend, zrecv, dsend, drecv,
    ysend_sem, yrecv_sem, zsend_sem, zrecv_sem, dsend_sem, drecv_sem, load_sem,
):
    species, xs, ys, lanes = cells.shape
    count = ny * nz
    gy, gz = lax.axis_index("gy"), lax.axis_index("gz")
    me = gy * nz + gz
    low, high = TOP - 1, TOP + ys
    halo_rounds = ITERS + 1

    load = pltpu.make_async_copy(state_ref.at[0], cells, load_sem)
    load.start()

    def peer(step):
        other = lax.rem(me + step, count)
        return {"gy": lax.div(other, nz), "gz": lax.rem(other, nz)}

    barrier = pltpu.get_barrier_semaphore()
    for step in range(1, count):
        pl.semaphore_signal(
            barrier, inc=1, device_id=peer(step), device_id_type=pl.DeviceIdType.MESH
        )

    slab = jnp.zeros((ys, lanes), jnp.float32)
    for k in range(species):
        for edge in (0, xs + 1):
            where = k * (xs + 2) + edge
            padded[where, TOP:high, :] = slab
            for j in range(ITERS):
                basis[j, where, TOP:high, :] = slab
    for side, outermost in ((0, gy == 0), (1, gy == ny - 1)):
        @pl.when(outermost)
        def _():
            for r in range(halo_rounds):
                yrecv[r, side] = jnp.zeros(yrecv.shape[2:], jnp.float32)
    for side, outermost in ((0, gz == 0), (1, gz == nz - 1)):
        @pl.when(outermost)
        def _():
            for r in range(halo_rounds):
                zrecv[r, side] = jnp.zeros(zrecv.shape[2:], jnp.float32)

    lane = lax.broadcasted_iota(jnp.int32, (ys, lanes), 1)
    odd = lax.rem(lane, 2) == 1
    first, last = lane == 0, lane == lanes - 1

    def halo_copies(r):
        listed = []
        for side, there, inside in ((0, 1, gy > 0), (1, 0, gy < ny - 1)):
            listed.append((inside, gy < ny - 1 if side == 0 else gy > 0,
                pltpu.make_async_remote_copy(
                    src_ref=ysend.at[r, side], dst_ref=yrecv.at[r, there],
                    send_sem=ysend_sem.at[r, side], recv_sem=yrecv_sem.at[r, there],
                    device_id={"gy": gy - 1 if side == 0 else gy + 1},
                    device_id_type=pl.DeviceIdType.MESH)))
        for side, there, inside in ((0, 1, gz > 0), (1, 0, gz < nz - 1)):
            listed.append((inside, gz < nz - 1 if side == 0 else gz > 0,
                pltpu.make_async_remote_copy(
                    src_ref=zsend.at[r], dst_ref=zrecv.at[r, there],
                    send_sem=zsend_sem.at[r, side], recv_sem=zrecv_sem.at[r, there],
                    device_id={"gz": gz - 1 if side == 0 else gz + 1},
                    device_id_type=pl.DeviceIdType.MESH)))
        return listed

    def start_halo(r):
        for inside, _, copy in halo_copies(r):
            @pl.when(inside)
            def _():
                copy.start()

    def finish_halo(r):
        for _, arriving, copy in halo_copies(r):
            @pl.when(arriving)
            def _():
                copy.wait_recv()
        return jnp.where(odd, zrecv[r, 0], pltpu.roll(zrecv[r, 1], lanes - 2, 1))

    def slot(k, x):
        return k * (xs + 2) + x + 1, k * xs + x

    def pack(zpack, block, r, k, x):
        _, j = slot(k, x)
        ysend[r, 0, pl.ds(j, 1), :] = block[0:1, :]
        ysend[r, 1, pl.ds(j, 1), :] = block[ys - 1 : ys, :]
        turned = pltpu.roll(block, 2 * j, 1)
        here = (lane == 2 * j) | (lane == lax.rem(2 * j + lanes - 1, lanes))
        return jnp.where(here, turned, zpack)

    def beside(ref, lead, zhalo, k, x):
        i, j = slot(k, x)
        at = lambda a, b: ref[lead + (a, slice(b, b + ys), slice(None))]
        here = at(i, TOP)
        edge = pltpu.roll(zhalo, lax.rem(lanes + 1 - 2 * j + lanes, lanes), 1)
        before = jnp.where(first, edge, pltpu.roll(here, 1, 1))
        after = jnp.where(last, edge, pltpu.roll(here, lanes - 1, 1))
        return (here, (at(i - 1, TOP), at(i + 1, TOP)), (at(i, TOP - 1), at(i, TOP + 1)),
                (before, after))

    def fold(value):
        total = value[0:8]
        for row in range(8, ys, 8):
            total = total + value[row : row + 8]
        return total

    load.wait()

    def take(x, zpack):
        for k in range(species):
            block = cells[k, x]
            padded[slot(k, x)[0], TOP:high, :] = block
            zpack = pack(zpack, block, 0, k, x)
        return zpack

    zsend[0] = lax.fori_loop(0, xs, take, jnp.zeros((ys, lanes), jnp.float32))
    pl.semaphore_wait(barrier, count - 1)
    start_halo(0)

    member = set_ref[0]
    courant = [courant_ref[member, d] for d in range(3)]
    strength = [diffuse_ref[member, k] for k in range(species)]
    rates = [[react_ref[member, k, l] for l in range(species)] for k in range(species)]
    coupling = [quad_ref[member, k] for k in range(species)]
    ahead = [jnp.maximum(c, 0.0) for c in courant]
    back = [jnp.minimum(c, 0.0) for c in courant]
    keep = 1.0
    for d in range(3):
        keep = keep - ahead[d] + back[d]

    zhalo = finish_halo(0)

    def set_rows(ref, lead, r, k, x):
        i, j = slot(k, x)
        ref[lead + (i, slice(low, low + 1), slice(None))] = yrecv[r, 0, pl.ds(j, 1), :]
        ref[lead + (i, slice(high, high + 1), slice(None))] = yrecv[r, 1, pl.ds(j, 1), :]

    def explicit(x, zpack):
        near = []
        for k in range(species):
            set_rows(padded, (), 0, k, x)
        for k in range(species):
            near.append(beside(padded, (), zhalo, k, x))
        a, b = near[0][0], near[1][0]
        coupled = a * b / (1.0 + a * a + b * b)
        for k in range(species):
            here = near[k][0]
            total = keep * here
            for d in range(3):
                total = total + ahead[d] * near[k][1 + d][0] - back[d] * near[k][1 + d][1]
            for l in range(species):
                total = total + rates[k][l] * near[l][0]
            total = total + coupling[k] * coupled
            basis[0, slot(k, x)[0], TOP:high, :] = total
            zpack = pack(zpack, total, 1, k, x)
        return zpack

    zsend[1] = lax.fori_loop(0, xs, explicit, jnp.zeros((ys, lanes), jnp.float32))
    start_halo(1)
    halos = [finish_halo(1)]

    def rows0(x, carry):
        for k in range(species):
            set_rows(basis, (0,), 1, k, x)
        return carry

    lax.fori_loop(0, xs, rows0, 0)

    def total_of(grid, row):
        return jnp.sum(grid[row : row + 1, :], axis=1, keepdims=True)

    cosines, sines, triangle = [], [], []
    target = None

    def rotate(entries, column):
        for earlier in range(column):
            rotated = cosines[earlier] * entries[earlier] + sines[earlier] * entries[earlier + 1]
            entries[earlier + 1] = (
                cosines[earlier] * entries[earlier + 1] - sines[earlier] * entries[earlier]
            )
            entries[earlier] = rotated
        radius = jnp.sqrt(
            entries[column] * entries[column] + entries[column + 1] * entries[column + 1]
        )
        cosine, sine = entries[column] / radius, entries[column + 1] / radius
        cosines.append(cosine)
        sines.append(sine)
        triangle.append(entries[:column] + [radius])
        target.append(-sine * target[column])
        target[column] = cosine * target[column]

    pending = None
    inverse_beta = None
    for column in range(ITERS):
        more = column + 1 < ITERS
        r = column + 2
        zhalo = halos[column]
        products = column + 1 + (2 if column == 0 else 1)

        def implicit(x, carry):
            zpack, sums = carry[0], list(carry[1:])
            for k in range(species):
                here, nearx, neary, nearz = beside(basis, (column,), zhalo, k, x)
                around = nearx[0] + nearx[1] + (neary[0] + neary[1]) + (nearz[0] + nearz[1])
                made = (1.0 + 6.0 * strength[k]) * here - strength[k] * around
                i = slot(k, x)[0]
                image[i, TOP:high, :] = made
                if more:
                    zpack = pack(zpack, made, r, k, x)
                for earlier in range(column):
                    sums[earlier] = sums[earlier] + fold(basis[earlier, i, TOP:high, :] * made)
                sums[column] = sums[column] + fold(here * made)
                sums[column + 1] = sums[column + 1] + fold(made * made)
                if column == 0:
                    sums[2] = sums[2] + fold(here * here)
            return (zpack, *sums)

        zero = jnp.zeros((8, lanes), jnp.float32)
        result = lax.fori_loop(
            0, xs, implicit, (jnp.zeros((ys, lanes), jnp.float32),) + (zero,) * products
        )
        rows = [jnp.sum(part, axis=0, keepdims=True) for part in result[1:]]
        mine = jnp.zeros((8, lanes), jnp.float32)
        row_of = lax.broadcasted_iota(jnp.int32, (8, lanes), 0)
        for p in range(products):
            mine = jnp.where(row_of == p, rows[p], mine)
        dsend[column] = mine
        for step in range(1, count):
            pltpu.make_async_remote_copy(
                src_ref=dsend.at[column], dst_ref=drecv.at[column, me],
                send_sem=dsend_sem.at[column], recv_sem=drecv_sem.at[column],
                device_id=peer(step), device_id_type=pl.DeviceIdType.MESH,
            ).start()
        if more:
            zsend[r] = result[0]
            start_halo(r)
        drecv[column, me] = mine
        if pending is not None:
            rotate(*pending)
        others = drecv.at[column, pl.ds(0, count - 1)]
        pltpu.make_async_copy(others, others, drecv_sem.at[column]).wait()
        grid = drecv[column, 0]
        for other in range(1, count):
            grid = grid + drecv[column, other]
        sums = [total_of(grid, p) for p in range(products)]
        if column == 0:
            beta = jnp.sqrt(sums[2])
            inverse_beta = 1.0 / beta
            target = [beta]
            square = inverse_beta * inverse_beta
            projections = [sums[0] * square]
            length_sq = sums[1] * square
        else:
            projections = [sums[0] * inverse_beta] + sums[1 : column + 1]
            length_sq = sums[column + 1]
        kept = projections[0] * projections[0]
        for value in projections[1:]:
            kept = kept + value * value
        norm_next = jnp.sqrt(length_sq - kept)
        pending = (projections + [norm_next], column)
        if not more:
            break
        inverse = 1.0 / norm_next
        gain = inverse if column else inverse * inverse_beta
        gains = [-(projections[0] * inverse) * inverse_beta] + [
            -(value * inverse) for value in projections[1:]
        ]
        zhalo_new = finish_halo(r) * gain
        for earlier in range(column + 1):
            zhalo_new = zhalo_new + halos[earlier] * gains[earlier]
        halos.append(zhalo_new)
        wide = jnp.broadcast_to(gain, (ys, lanes))
        wides = [jnp.broadcast_to(g, (ys, lanes)) for g in gains]

        def combine(x, carry):
            for k in range(species):
                i, j = slot(k, x)
                total = image[i, TOP:high, :] * wide
                below = yrecv[r, 0, pl.ds(j, 1), :] * wide[0:1]
                above = yrecv[r, 1, pl.ds(j, 1), :] * wide[0:1]
                for earlier in range(column + 1):
                    total = total + basis[earlier, i, TOP:high, :] * wides[earlier]
                    below = below + basis[earlier, i, low : low + 1, :] * wides[earlier][0:1]
                    above = above + basis[earlier, i, high : high + 1, :] * wides[earlier][0:1]
                basis[column + 1, i, TOP:high, :] = total
                basis[column + 1, i, low : low + 1, :] = below
                basis[column + 1, i, high : high + 1, :] = above
            return carry

        lax.fori_loop(0, xs, combine, 0)

    rotate(*pending)
    coeffs = [None] * ITERS
    for column in reversed(range(ITERS)):
        running = target[column]
        for further in range(column + 1, ITERS):
            running = running - triangle[further][column] * coeffs[further]
        coeffs[column] = running / triangle[column][column]
    coeffs[0] = coeffs[0] * inverse_beta
    wides = [jnp.broadcast_to(c, (ys, lanes)) for c in coeffs]

    def finish(x, carry):
        for k in range(species):
            i = slot(k, x)[0]
            total = basis[0, i, TOP:high, :] * wides[0]
            for column in range(1, ITERS):
                total = total + basis[column, i, TOP:high, :] * wides[column]
            out_ref[0, k, x] = total
        return carry

    lax.fori_loop(0, xs, finish, 0)

    for r in range(halo_rounds):
        for inside, _, copy in halo_copies(r):
            @pl.when(inside)
            def _():
                copy.wait_send()
    for column in range(ITERS):
        others = drecv.at[column, pl.ds(0, count - 1)]
        pltpu.make_async_copy(others, others, dsend_sem.at[column]).wait()


def shards(ny, nz, state, member_set, courant, diffusion, reaction, quadratic):
    _, species, xs, ys, lanes = state.shape
    blocks, tall = species * (xs + 2), TOP + ys + 8
    rounds, count = ITERS + 1, ny * nz
    f32 = jnp.float32
    smem = pl.BlockSpec(memory_space=pltpu.SMEM)
    return pl.pallas_call(
        functools.partial(kernel, ny, nz),
        out_shape=jax.ShapeDtypeStruct(state.shape, f32),
        in_specs=[pl.BlockSpec(memory_space=pl.ANY)] + [smem] * 5,
        out_specs=pl.BlockSpec(memory_space=pltpu.VMEM),
        scratch_shapes=[
            pltpu.VMEM((species, xs, ys, lanes), f32),
            pltpu.VMEM((blocks, tall, lanes), f32),
            pltpu.VMEM((blocks, tall, lanes), f32),
            pltpu.VMEM((ITERS, blocks, tall, lanes), f32),
            pltpu.VMEM((rounds, 2, species * xs, lanes), f32),
            pltpu.VMEM((rounds, 2, species * xs, lanes), f32),
            pltpu.VMEM((rounds, ys, lanes), f32),
            pltpu.VMEM((rounds, 2, ys, lanes), f32),
            pltpu.VMEM((ITERS, 8, lanes), f32),
            pltpu.VMEM((ITERS, count, 8, lanes), f32),
            pltpu.SemaphoreType.DMA((rounds, 2)),
            pltpu.SemaphoreType.DMA((rounds, 2)),
            pltpu.SemaphoreType.DMA((rounds, 2)),
            pltpu.SemaphoreType.DMA((rounds, 2)),
            pltpu.SemaphoreType.DMA((ITERS,)),
            pltpu.SemaphoreType.DMA((ITERS,)),
            pltpu.SemaphoreType.DMA,
        ],
        compiler_params=pltpu.CompilerParams(collective_id=0, has_side_effects=True),
    )(state, member_set, courant, diffusion, reaction, quadratic)


def solution(mesh):
    return jax.shard_map(
        functools.partial(shards, mesh.shape["gy"], mesh.shape["gz"]),
        mesh=mesh,
        in_specs=(P("ens", None, None, "gy", "gz"), P("ens"), P(), P(), P(), P()),
        out_specs=P("ens", None, None, "gy", "gz"),
        check_vma=False,
    )
```

```python
import functools

import jax
import jax.numpy as jnp
from jax import lax
from jax.experimental import pallas as pl
from jax.experimental.pallas import tpu as pltpu
from jax.sharding import PartitionSpec as P

ITERS = 4
TOP = 8


def kernel(
    ny, nz,
    state_ref, set_ref, courant_hbm, diffuse_hbm, react_hbm, quad_hbm,
    out_ref,
    courant_ref, diffuse_ref, react_ref, quad_ref, table_sem,
    cells, padded, image, basis,
    ysend, yrecv, zsend, zrecv, dsend, drecv,
    ysend_sem, yrecv_sem, zsend_sem, zrecv_sem, dsend_sem, drecv_sem, load_sem,
):
    species, xs, ys, lanes = cells.shape
    count = ny * nz
    gy, gz = lax.axis_index("gy"), lax.axis_index("gz")
    me = gy * nz + gz
    low, high = TOP - 1, TOP + ys
    halo_rounds = ITERS + 1

    load = pltpu.make_async_copy(state_ref.at[0], cells, load_sem)
    load.start()
    tables = [
        pltpu.make_async_copy(source, target, table_sem.at[n])
        for n, (source, target) in enumerate((
            (courant_hbm, courant_ref), (diffuse_hbm, diffuse_ref), (react_hbm, react_ref), (quad_hbm, quad_ref)))
    ]
    for table in tables:
        table.start()

    def peer(step):
        other = lax.rem(me + step, count)
        return {"gy": lax.div(other, nz), "gz": lax.rem(other, nz)}

    barrier = pltpu.get_barrier_semaphore()
    for step in range(1, count):
        pl.semaphore_signal(
            barrier, inc=1, device_id=peer(step), device_id_type=pl.DeviceIdType.MESH
        )

    slab = jnp.zeros((ys, lanes), jnp.float32)
    for k in range(species):
        for edge in (0, xs + 1):
            where = k * (xs + 2) + edge
            padded[where, TOP:high, :] = slab
            for j in range(ITERS):
                basis[j, where, TOP:high, :] = slab
    for side, outermost in ((0, gy == 0), (1, gy == ny - 1)):
        @pl.when(outermost)
        def _():
            for r in range(halo_rounds):
                yrecv[r, side] = jnp.zeros(yrecv.shape[2:], jnp.float32)
    for side, outermost in ((0, gz == 0), (1, gz == nz - 1)):
        @pl.when(outermost)
        def _():
            for r in range(halo_rounds):
                zrecv[r, side] = jnp.zeros(zrecv.shape[2:], jnp.float32)

    lane = lax.broadcasted_iota(jnp.int32, (ys, lanes), 1)
    odd = lax.rem(lane, 2) == 1
    first, last = lane == 0, lane == lanes - 1

    def halo_copies(r):
        listed = []
        for side, there, inside in ((0, 1, gy > 0), (1, 0, gy < ny - 1)):
            listed.append((inside, gy < ny - 1 if side == 0 else gy > 0,
                pltpu.make_async_remote_copy(
                    src_ref=ysend.at[r, side], dst_ref=yrecv.at[r, there],
                    send_sem=ysend_sem.at[r, side], recv_sem=yrecv_sem.at[r, there],
                    device_id={"gy": gy - 1 if side == 0 else gy + 1},
                    device_id_type=pl.DeviceIdType.MESH)))
        for side, there, inside in ((0, 1, gz > 0), (1, 0, gz < nz - 1)):
            listed.append((inside, gz < nz - 1 if side == 0 else gz > 0,
                pltpu.make_async_remote_copy(
                    src_ref=zsend.at[r], dst_ref=zrecv.at[r, there],
                    send_sem=zsend_sem.at[r, side], recv_sem=zrecv_sem.at[r, there],
                    device_id={"gz": gz - 1 if side == 0 else gz + 1},
                    device_id_type=pl.DeviceIdType.MESH)))
        return listed

    def start_halo(r):
        for inside, _, copy in halo_copies(r):
            @pl.when(inside)
            def _():
                copy.start()

    def finish_halo(r):
        for _, arriving, copy in halo_copies(r):
            @pl.when(arriving)
            def _():
                copy.wait_recv()
        return jnp.where(odd, zrecv[r, 0], pltpu.roll(zrecv[r, 1], lanes - 2, 1))

    def slot(k, x):
        return k * (xs + 2) + x + 1, k * xs + x

    def pack(zpack, block, r, k, x):
        _, j = slot(k, x)
        ysend[r, 0, pl.ds(j, 1), :] = block[0:1, :]
        ysend[r, 1, pl.ds(j, 1), :] = block[ys - 1 : ys, :]
        turned = pltpu.roll(block, 2 * j, 1)
        here = (lane == 2 * j) | (lane == lax.rem(2 * j + lanes - 1, lanes))
        return jnp.where(here, turned, zpack)

    def beside(ref, lead, zhalo, k, x):
        i, j = slot(k, x)
        at = lambda a, b: ref[lead + (a, slice(b, b + ys), slice(None))]
        here = at(i, TOP)
        edge = pltpu.roll(zhalo, lax.rem(lanes + 1 - 2 * j + lanes, lanes), 1)
        before = jnp.where(first, edge, pltpu.roll(here, 1, 1))
        after = jnp.where(last, edge, pltpu.roll(here, lanes - 1, 1))
        return (here, (at(i - 1, TOP), at(i + 1, TOP)), (at(i, TOP - 1), at(i, TOP + 1)),
                (before, after))

    def fold(value):
        total = value[0:8]
        for row in range(8, ys, 8):
            total = total + value[row : row + 8]
        return total

    load.wait()

    def take(x, zpack):
        for k in range(species):
            block = cells[k, x]
            padded[slot(k, x)[0], TOP:high, :] = block
            zpack = pack(zpack, block, 0, k, x)
        return zpack

    zsend[0] = lax.fori_loop(0, xs, take, jnp.zeros((ys, lanes), jnp.float32), unroll=2)
    pl.semaphore_wait(barrier, count - 1)
    start_halo(0)

    for table in tables:
        table.wait()
    member = set_ref[0]
    courant = [courant_ref[d, member] for d in range(3)]
    strength = [diffuse_ref[k, member] for k in range(species)]
    rates = [[react_ref[k, l, member] for l in range(species)] for k in range(species)]
    coupling = [quad_ref[k, member] for k in range(species)]
    ahead = [jnp.maximum(c, 0.0) for c in courant]
    back = [jnp.minimum(c, 0.0) for c in courant]
    keep = 1.0
    for d in range(3):
        keep = keep - ahead[d] + back[d]

    zhalo = finish_halo(0)

    def set_rows(ref, lead, r, k, x):
        i, j = slot(k, x)
        ref[lead + (i, slice(low, low + 1), slice(None))] = yrecv[r, 0, pl.ds(j, 1), :]
        ref[lead + (i, slice(high, high + 1), slice(None))] = yrecv[r, 1, pl.ds(j, 1), :]

    def explicit(x, zpack):
        near = []
        for k in range(species):
            set_rows(padded, (), 0, k, x)
        for k in range(species):
            near.append(beside(padded, (), zhalo, k, x))
        a, b = near[0][0], near[1][0]
        coupled = a * b / (1.0 + a * a + b * b)
        for k in range(species):
            here = near[k][0]
            total = keep * here
            for d in range(3):
                total = total + ahead[d] * near[k][1 + d][0] - back[d] * near[k][1 + d][1]
            for l in range(species):
                total = total + rates[k][l] * near[l][0]
            total = total + coupling[k] * coupled
            basis[0, slot(k, x)[0], TOP:high, :] = total
            zpack = pack(zpack, total, 1, k, x)
        return zpack

    zsend[1] = lax.fori_loop(0, xs, explicit, jnp.zeros((ys, lanes), jnp.float32), unroll=2)
    start_halo(1)
    halos = [finish_halo(1)]

    def rows0(x, carry):
        for k in range(species):
            set_rows(basis, (0,), 1, k, x)
        return carry

    lax.fori_loop(0, xs, rows0, 0, unroll=4)

    cosines, sines, triangle = [], [], []
    target = None

    def rotate(entries, column):
        for earlier in range(column):
            rotated = cosines[earlier] * entries[earlier] + sines[earlier] * entries[earlier + 1]
            entries[earlier + 1] = (
                cosines[earlier] * entries[earlier + 1] - sines[earlier] * entries[earlier]
            )
            entries[earlier] = rotated
        radius = jnp.sqrt(
            entries[column] * entries[column] + entries[column + 1] * entries[column + 1]
        )
        cosine, sine = entries[column] / radius, entries[column + 1] / radius
        cosines.append(cosine)
        sines.append(sine)
        triangle.append(entries[:column] + [radius])
        target.append(-sine * target[column])
        target[column] = cosine * target[column]

    pending = None
    inverse_beta = None
    for column in range(ITERS):
        more = column + 1 < ITERS
        r = column + 2
        zhalo = halos[column]
        products = column + 1 + (2 if column == 0 else 1)

        def implicit(x, carry):
            zpack, sums = carry[0], list(carry[1:])
            for k in range(species):
                here, nearx, neary, nearz = beside(basis, (column,), zhalo, k, x)
                around = nearx[0] + nearx[1] + (neary[0] + neary[1]) + (nearz[0] + nearz[1])
                made = (1.0 + 6.0 * strength[k]) * here - strength[k] * around
                i = slot(k, x)[0]
                image[i, TOP:high, :] = made
                if more:
                    zpack = pack(zpack, made, r, k, x)
                for earlier in range(column):
                    sums[earlier] = sums[earlier] + fold(basis[earlier, i, TOP:high, :] * made)
                sums[column] = sums[column] + fold(here * made)
                sums[column + 1] = sums[column + 1] + fold(made * made)
                if column == 0:
                    sums[2] = sums[2] + fold(here * here)
            return (zpack, *sums)

        zero = jnp.zeros((8, lanes), jnp.float32)
        result = lax.fori_loop(
            0, xs, implicit, (jnp.zeros((ys, lanes), jnp.float32),) + (zero,) * products,
            unroll=2,
        )
        rows = [jnp.sum(part, axis=0, keepdims=True) for part in result[1:]]
        mine = jnp.zeros((1, lanes), jnp.float32)
        for p in range(products):
            mine = jnp.where(lane[0:1] == p, jnp.sum(rows[p], axis=1, keepdims=True), mine)
        dsend[column] = mine
        for step in range(1, count):
            pltpu.make_async_remote_copy(
                src_ref=dsend.at[column], dst_ref=drecv.at[column, me],
                send_sem=dsend_sem.at[column], recv_sem=drecv_sem.at[column],
                device_id=peer(step), device_id_type=pl.DeviceIdType.MESH,
            ).start()
        if more:
            zsend[r] = result[0]
            start_halo(r)
        drecv[column, me] = mine
        if pending is not None:
            rotate(*pending)
        others = drecv.at[column, pl.ds(0, count - 1)]
        pltpu.make_async_copy(others, others, drecv_sem.at[column]).wait()
        grid = drecv[column, 0]
        for other in range(1, count):
            grid = grid + drecv[column, other]
        sums = [grid[:, p : p + 1] for p in range(products)]
        if column == 0:
            beta = jnp.sqrt(sums[2])
            inverse_beta = 1.0 / beta
            target = [beta]
            square = inverse_beta * inverse_beta
            projections = [sums[0] * square]
            length_sq = sums[1] * square
        else:
            projections = [sums[0] * inverse_beta] + sums[1 : column + 1]
            length_sq = sums[column + 1]
        kept = projections[0] * projections[0]
        for value in projections[1:]:
            kept = kept + value * value
        norm_next = jnp.sqrt(length_sq - kept)
        pending = (projections + [norm_next], column)
        if not more:
            break
        inverse = 1.0 / norm_next
        gain = inverse if column else inverse * inverse_beta
        gains = [-(projections[0] * inverse) * inverse_beta] + [
            -(value * inverse) for value in projections[1:]
        ]
        zhalo_new = finish_halo(r) * gain
        for earlier in range(column + 1):
            zhalo_new = zhalo_new + halos[earlier] * gains[earlier]
        halos.append(zhalo_new)
        wide = jnp.broadcast_to(gain, (ys, lanes))
        wides = [jnp.broadcast_to(g, (ys, lanes)) for g in gains]

        def combine(x, carry):
            for k in range(species):
                i, j = slot(k, x)
                total = image[i, TOP:high, :] * wide
                below = yrecv[r, 0, pl.ds(j, 1), :] * wide[0:1]
                above = yrecv[r, 1, pl.ds(j, 1), :] * wide[0:1]
                for earlier in range(column + 1):
                    total = total + basis[earlier, i, TOP:high, :] * wides[earlier]
                    below = below + basis[earlier, i, low : low + 1, :] * wides[earlier][0:1]
                    above = above + basis[earlier, i, high : high + 1, :] * wides[earlier][0:1]
                basis[column + 1, i, TOP:high, :] = total
                basis[column + 1, i, low : low + 1, :] = below
                basis[column + 1, i, high : high + 1, :] = above
            return carry

        lax.fori_loop(0, xs, combine, 0, unroll=2)

    rotate(*pending)
    coeffs = [None] * ITERS
    for column in reversed(range(ITERS)):
        running = target[column]
        for further in range(column + 1, ITERS):
            running = running - triangle[further][column] * coeffs[further]
        coeffs[column] = running / triangle[column][column]
    coeffs[0] = coeffs[0] * inverse_beta
    wides = [jnp.broadcast_to(c, (ys, lanes)) for c in coeffs]

    def finish(x, carry):
        for k in range(species):
            i = slot(k, x)[0]
            total = basis[0, i, TOP:high, :] * wides[0]
            for column in range(1, ITERS):
                total = total + basis[column, i, TOP:high, :] * wides[column]
            out_ref[0, k, x] = total
        return carry

    lax.fori_loop(0, xs, finish, 0, unroll=2)

    for r in range(halo_rounds):
        for inside, _, copy in halo_copies(r):
            @pl.when(inside)
            def _():
                copy.wait_send()
    for column in range(ITERS):
        others = drecv.at[column, pl.ds(0, count - 1)]
        pltpu.make_async_copy(others, others, dsend_sem.at[column]).wait()


def shards(ny, nz, state, member_set, courant, diffusion, reaction, quadratic):
    _, species, xs, ys, lanes = state.shape
    blocks, tall = species * (xs + 2), TOP + ys + 8
    rounds, count = ITERS + 1, ny * nz
    f32 = jnp.float32
    anywhere = pl.BlockSpec(memory_space=pl.ANY)
    tables = (courant.T, diffusion.T, jnp.transpose(reaction, (1, 2, 0)), quadratic.T)
    return pl.pallas_call(
        functools.partial(kernel, ny, nz),
        out_shape=pltpu.VMEM(state.shape, f32),
        in_specs=[anywhere, pl.BlockSpec(memory_space=pltpu.SMEM)] + [anywhere] * len(tables),
        out_specs=pl.BlockSpec(memory_space=pltpu.VMEM),
        scratch_shapes=[pltpu.SMEM(table.shape, table.dtype) for table in tables] + [
            pltpu.SemaphoreType.DMA((len(tables),)),
            pltpu.VMEM((species, xs, ys, lanes), f32),
            pltpu.VMEM((blocks, tall, lanes), f32),
            pltpu.VMEM((blocks, tall, lanes), f32),
            pltpu.VMEM((ITERS, blocks, tall, lanes), f32),
            pltpu.VMEM((rounds, 2, species * xs, lanes), f32),
            pltpu.VMEM((rounds, 2, species * xs, lanes), f32),
            pltpu.VMEM((rounds, ys, lanes), f32),
            pltpu.VMEM((rounds, 2, ys, lanes), f32),
            pltpu.VMEM((ITERS, 1, lanes), f32),
            pltpu.VMEM((ITERS, count, 1, lanes), f32),
            pltpu.SemaphoreType.DMA((rounds, 2)),
            pltpu.SemaphoreType.DMA((rounds, 2)),
            pltpu.SemaphoreType.DMA((rounds, 2)),
            pltpu.SemaphoreType.DMA((rounds, 2)),
            pltpu.SemaphoreType.DMA((ITERS,)),
            pltpu.SemaphoreType.DMA((ITERS,)),
            pltpu.SemaphoreType.DMA,
        ],
        compiler_params=pltpu.CompilerParams(collective_id=0, has_side_effects=True),
    )(state, member_set, *tables)


def solution(mesh):
    return jax.shard_map(
        functools.partial(shards, mesh.shape["gy"], mesh.shape["gz"]),
        mesh=mesh,
        in_specs=(P("ens", None, None, "gy", "gz"), P("ens"), P(), P(), P(), P()),
        out_specs=P("ens", None, None, "gy", "gz"),
        check_vma=False,
    )
```

```python
import functools

import jax
import jax.numpy as jnp
from jax import lax
from jax.experimental import pallas as pl
from jax.experimental.pallas import tpu as pltpu
from jax.sharding import PartitionSpec as P

ITERS = 4
TOP = 8


def kernel(
    ny, nz,
    state_ref, set_ref, courant_hbm, diffuse_hbm, react_hbm, quad_hbm,
    out_ref,
    courant_ref, diffuse_ref, react_ref, quad_ref, table_sem,
    cells, padded, further, images, basis,
    ysend, yrecv, zsend, zrecv, dsend, drecv,
    ysend_sem, yrecv_sem, zsend_sem, zrecv_sem, dsend_sem, drecv_sem, load_sem,
):
    species, xs, ys, lanes = cells.shape
    count = ny * nz
    gy, gz = lax.axis_index("gy"), lax.axis_index("gz")
    me = gy * nz + gz
    low, high = TOP - 1, TOP + ys
    halo_rounds = ITERS + 1

    load = pltpu.make_async_copy(state_ref.at[0], cells, load_sem)
    load.start()
    tables = [
        pltpu.make_async_copy(source, target, table_sem.at[n])
        for n, (source, target) in enumerate((
            (courant_hbm, courant_ref), (diffuse_hbm, diffuse_ref), (react_hbm, react_ref), (quad_hbm, quad_ref)))
    ]
    for table in tables:
        table.start()

    def peer(step):
        other = lax.rem(me + step, count)
        return {"gy": lax.div(other, nz), "gz": lax.rem(other, nz)}

    barrier = pltpu.get_barrier_semaphore()
    for step in range(1, count):
        pl.semaphore_signal(
            barrier, inc=1, device_id=peer(step), device_id_type=pl.DeviceIdType.MESH
        )

    slab = jnp.zeros((ys, lanes), jnp.float32)
    for k in range(species):
        for edge in (0, xs + 1):
            where = k * (xs + 2) + edge
            padded[where, TOP:high, :] = slab
            for j in range(ITERS - 1):
                images[j, where, TOP:high, :] = slab
            basis[0, where, TOP:high, :] = slab
    for side, outermost in ((0, gy == 0), (1, gy == ny - 1)):
        @pl.when(outermost)
        def _():
            for r in range(halo_rounds):
                yrecv[r, side] = jnp.zeros(yrecv.shape[2:], jnp.float32)
    for side, outermost in ((0, gz == 0), (1, gz == nz - 1)):
        @pl.when(outermost)
        def _():
            for r in range(halo_rounds):
                zrecv[r, side] = jnp.zeros(zrecv.shape[2:], jnp.float32)

    lane = lax.broadcasted_iota(jnp.int32, (ys, lanes), 1)
    odd = lax.rem(lane, 2) == 1
    first, last = lane == 0, lane == lanes - 1

    def halo_copies(r):
        listed = []
        for side, there, inside in ((0, 1, gy > 0), (1, 0, gy < ny - 1)):
            listed.append((inside, gy < ny - 1 if side == 0 else gy > 0,
                pltpu.make_async_remote_copy(
                    src_ref=ysend.at[r, side], dst_ref=yrecv.at[r, there],
                    send_sem=ysend_sem.at[r, side], recv_sem=yrecv_sem.at[r, there],
                    device_id={"gy": gy - 1 if side == 0 else gy + 1},
                    device_id_type=pl.DeviceIdType.MESH)))
        for side, there, inside in ((0, 1, gz > 0), (1, 0, gz < nz - 1)):
            listed.append((inside, gz < nz - 1 if side == 0 else gz > 0,
                pltpu.make_async_remote_copy(
                    src_ref=zsend.at[r], dst_ref=zrecv.at[r, there],
                    send_sem=zsend_sem.at[r, side], recv_sem=zrecv_sem.at[r, there],
                    device_id={"gz": gz - 1 if side == 0 else gz + 1},
                    device_id_type=pl.DeviceIdType.MESH)))
        return listed

    def start_halo(r):
        for inside, _, copy in halo_copies(r):
            @pl.when(inside)
            def _():
                copy.start()

    def finish_halo(r):
        for _, arriving, copy in halo_copies(r):
            @pl.when(arriving)
            def _():
                copy.wait_recv()
        return jnp.where(odd, zrecv[r, 0], pltpu.roll(zrecv[r, 1], lanes - 2, 1))

    def slot(k, x):
        return k * (xs + 2) + x + 1, k * xs + x

    def pack(zpack, block, r, k, x):
        _, j = slot(k, x)
        ysend[r, 0, pl.ds(j, 1), :] = block[0:1, :]
        ysend[r, 1, pl.ds(j, 1), :] = block[ys - 1 : ys, :]
        turned = pltpu.roll(block, 2 * j, 1)
        here = (lane == 2 * j) | (lane == lax.rem(2 * j + lanes - 1, lanes))
        return jnp.where(here, turned, zpack)

    def beside(ref, lead, zhalo, k, x):
        i, j = slot(k, x)
        at = lambda a, b: ref[lead + (a, slice(b, b + ys), slice(None))]
        here = at(i, TOP)
        edge = pltpu.roll(zhalo, lax.rem(lanes + 1 - 2 * j + lanes, lanes), 1)
        before = jnp.where(first, edge, pltpu.roll(here, 1, 1))
        after = jnp.where(last, edge, pltpu.roll(here, lanes - 1, 1))
        return (here, (at(i - 1, TOP), at(i + 1, TOP)), (at(i, TOP - 1), at(i, TOP + 1)),
                (before, after))

    def fold(value):
        total = value[0:8]
        for row in range(8, ys, 8):
            total = total + value[row : row + 8]
        return total

    load.wait()

    def take(x, zpack):
        for k in range(species):
            block = cells[k, x]
            padded[slot(k, x)[0], TOP:high, :] = block
            zpack = pack(zpack, block, 0, k, x)
        return zpack

    zsend[0] = lax.fori_loop(0, xs, take, jnp.zeros((ys, lanes), jnp.float32), unroll=2)
    pl.semaphore_wait(barrier, count - 1)
    start_halo(0)

    for table in tables:
        table.wait()
    member = set_ref[0]
    courant = [courant_ref[d, member] for d in range(3)]
    strength = [diffuse_ref[k, member] for k in range(species)]
    rates = [[react_ref[k, l, member] for l in range(species)] for k in range(species)]
    coupling = [quad_ref[k, member] for k in range(species)]
    ahead = [jnp.maximum(c, 0.0) for c in courant]
    back = [jnp.minimum(c, 0.0) for c in courant]
    keep = 1.0
    for d in range(3):
        keep = keep - ahead[d] + back[d]

    zhalo = finish_halo(0)

    def set_rows(ref, lead, r, k, x):
        i, j = slot(k, x)
        ref[lead + (i, slice(low, low + 1), slice(None))] = yrecv[r, 0, pl.ds(j, 1), :]
        ref[lead + (i, slice(high, high + 1), slice(None))] = yrecv[r, 1, pl.ds(j, 1), :]

    def explicit(x, zpack):
        near = []
        for k in range(species):
            set_rows(padded, (), 0, k, x)
        for k in range(species):
            near.append(beside(padded, (), zhalo, k, x))
        a, b = near[0][0], near[1][0]
        coupled = a * b / (1.0 + a * a + b * b)
        for k in range(species):
            here = near[k][0]
            total = keep * here
            for d in range(3):
                total = total + ahead[d] * near[k][1 + d][0] - back[d] * near[k][1 + d][1]
            for l in range(species):
                total = total + rates[k][l] * near[l][0]
            total = total + coupling[k] * coupled
            basis[0, slot(k, x)[0], TOP:high, :] = total
            zpack = pack(zpack, total, 1, k, x)
        return zpack

    zsend[1] = lax.fori_loop(0, xs, explicit, jnp.zeros((ys, lanes), jnp.float32), unroll=2)
    start_halo(1)
    zhalo = finish_halo(1)

    def rows0(x, carry):
        for k in range(species):
            set_rows(basis, (0,), 1, k, x)
        return carry

    lax.fori_loop(0, xs, rows0, 0, unroll=4)

    cosines, sines, triangle = [], [], []
    target = None

    def rotate(entries, column):
        for earlier in range(column):
            rotated = cosines[earlier] * entries[earlier] + sines[earlier] * entries[earlier + 1]
            entries[earlier + 1] = (
                cosines[earlier] * entries[earlier + 1] - sines[earlier] * entries[earlier]
            )
            entries[earlier] = rotated
        radius = jnp.sqrt(
            entries[column] * entries[column] + entries[column + 1] * entries[column + 1]
        )
        cosine, sine = entries[column] / radius, entries[column + 1] / radius
        cosines.append(cosine)
        sines.append(sine)
        triangle.append(entries[:column] + [radius])
        target.append(-sine * target[column])
        target[column] = cosine * target[column]

    zero = jnp.zeros((8, lanes), jnp.float32)
    blank = jnp.zeros((ys, lanes), jnp.float32)

    def applied(ref, lead, k, x, halo):
        here, nearx, neary, nearz = beside(ref, lead, halo, k, x)
        around = nearx[0] + nearx[1] + (neary[0] + neary[1]) + (nearz[0] + nearz[1])
        return here, (1.0 + 6.0 * strength[k]) * here - strength[k] * around

    def share(column, parts):
        mine = jnp.zeros((1, lanes), jnp.float32)
        for p, part in enumerate(parts):
            row = jnp.sum(part, axis=0, keepdims=True)
            mine = jnp.where(lane[0:1] == p, jnp.sum(row, axis=1, keepdims=True), mine)
        dsend[column] = mine
        for step in range(1, count):
            pltpu.make_async_remote_copy(
                src_ref=dsend.at[column], dst_ref=drecv.at[column, me],
                send_sem=dsend_sem.at[column], recv_sem=drecv_sem.at[column],
                device_id=peer(step), device_id_type=pl.DeviceIdType.MESH,
            ).start()
        drecv[column, me] = mine

    def gathered(column, products):
        others = drecv.at[column, pl.ds(0, count - 1)]
        pltpu.make_async_copy(others, others, drecv_sem.at[column]).wait()
        grid = drecv[column, 0]
        for other in range(1, count):
            grid = grid + drecv[column, other]
        return [grid[:, p : p + 1] for p in range(products)]

    def implicit(x, carry):
        zpack, cross, square, own = carry
        for k in range(species):
            here, made = applied(basis, (0,), k, x, zhalo)
            images[0, slot(k, x)[0], TOP:high, :] = made
            zpack = pack(zpack, made, 2, k, x)
            cross = cross + fold(here * made)
            square = square + fold(made * made)
            own = own + fold(here * here)
        return zpack, cross, square, own

    zpack, *parts = lax.fori_loop(0, xs, implicit, (blank, zero, zero, zero), unroll=2)
    share(0, parts)
    zsend[2] = zpack
    start_halo(2)
    halos = [finish_halo(2)]

    def rows1(x, carry):
        for k in range(species):
            set_rows(images, (0,), 2, k, x)
        return carry

    lax.fori_loop(0, xs, rows1, 0, unroll=4)

    pending = None
    for column in range(ITERS):
        more = column + 1 < ITERS
        wider = column + 2 < ITERS
        r = column + 3
        if more:
            def again(x, zpack):
                for k in range(species):
                    _, made = applied(images, (column,), k, x, halos[column])
                    further[slot(k, x)[0]] = made
                    if wider:
                        zpack = pack(zpack, made, r, k, x)
                return zpack

            zpack = lax.fori_loop(0, xs, again, blank, unroll=2)
            if wider:
                zsend[r] = zpack
                start_halo(r)
        if pending is not None:
            rotate(*pending)
        sums = gathered(column, 3 if column == 0 else column + 2)
        if column == 0:
            beta = jnp.sqrt(sums[2])
            inverse_beta = 1.0 / beta
            target = [beta]
            square = inverse_beta * inverse_beta
            projections = [sums[0] * square]
            length_sq = sums[1] * square
        else:
            projections = [sums[0] * inverse_beta] + sums[1 : column + 1]
            length_sq = sums[column + 1]
        kept = projections[0] * projections[0]
        for value in projections[1:]:
            kept = kept + value * value
        norm_next = jnp.sqrt(length_sq - kept)
        pending = (projections + [norm_next], column)
        if not more:
            break
        inverse = 1.0 / norm_next
        gain = inverse if column else inverse * inverse_beta
        gains = [-(projections[0] * inverse) * inverse_beta] + [
            -(value * inverse) for value in projections[1:]
        ]
        wide = jnp.broadcast_to(gain, (ys, lanes))
        wides = [jnp.broadcast_to(g, (ys, lanes)) for g in gains]

        def combine(x, sums):
            sums = list(sums)
            for k in range(species):
                i = slot(k, x)[0]
                olds = [basis[earlier, i, TOP:high, :] for earlier in range(column + 1)]
                vector = images[column, i, TOP:high, :] * wide
                made = further[i] * wide
                for earlier in range(column + 1):
                    vector = vector + olds[earlier] * wides[earlier]
                    made = made + images[earlier, i, TOP:high, :] * wides[earlier]
                basis[column + 1, i, TOP:high, :] = vector
                images[column + 1, i, TOP:high, :] = made
                for p, left in enumerate(olds + [vector, made]):
                    sums[p] = sums[p] + fold(left * made)
            return tuple(sums)

        share(column + 1, lax.fori_loop(0, xs, combine, (zero,) * (column + 3), unroll=2))
        if wider:
            fresh = finish_halo(r) * gain
            for earlier in range(column + 1):
                fresh = fresh + halos[earlier] * gains[earlier]
            halos.append(fresh)

            def borders(x, carry):
                for k in range(species):
                    i, j = slot(k, x)
                    for side, row in ((0, low), (1, high)):
                        line = yrecv[r, side, pl.ds(j, 1), :] * wide[0:1]
                        for earlier in range(column + 1):
                            line = line + images[earlier, i, row : row + 1, :] * wides[earlier][0:1]
                        images[column + 1, i, row : row + 1, :] = line
                return carry

            lax.fori_loop(0, xs, borders, 0, unroll=2)

    rotate(*pending)
    coeffs = [None] * ITERS
    for column in reversed(range(ITERS)):
        running = target[column]
        for further in range(column + 1, ITERS):
            running = running - triangle[further][column] * coeffs[further]
        coeffs[column] = running / triangle[column][column]
    coeffs[0] = coeffs[0] * inverse_beta
    wides = [jnp.broadcast_to(c, (ys, lanes)) for c in coeffs]

    def finish(x, carry):
        for k in range(species):
            i = slot(k, x)[0]
            total = basis[0, i, TOP:high, :] * wides[0]
            for column in range(1, ITERS):
                total = total + basis[column, i, TOP:high, :] * wides[column]
            out_ref[0, k, x] = total
        return carry

    lax.fori_loop(0, xs, finish, 0, unroll=2)

    for r in range(halo_rounds):
        for inside, _, copy in halo_copies(r):
            @pl.when(inside)
            def _():
                copy.wait_send()
    for column in range(ITERS):
        others = drecv.at[column, pl.ds(0, count - 1)]
        pltpu.make_async_copy(others, others, dsend_sem.at[column]).wait()


def shards(ny, nz, state, member_set, courant, diffusion, reaction, quadratic):
    _, species, xs, ys, lanes = state.shape
    blocks, tall = species * (xs + 2), TOP + ys + 8
    rounds, count = ITERS + 1, ny * nz
    f32 = jnp.float32
    anywhere = pl.BlockSpec(memory_space=pl.ANY)
    tables = (courant.T, diffusion.T, jnp.transpose(reaction, (1, 2, 0)), quadratic.T)
    return pl.pallas_call(
        functools.partial(kernel, ny, nz),
        out_shape=pltpu.VMEM(state.shape, f32),
        in_specs=[anywhere, pl.BlockSpec(memory_space=pltpu.SMEM)] + [anywhere] * len(tables),
        out_specs=pl.BlockSpec(memory_space=pltpu.VMEM),
        scratch_shapes=[pltpu.SMEM(table.shape, table.dtype) for table in tables] + [
            pltpu.SemaphoreType.DMA((len(tables),)),
            pltpu.VMEM((species, xs, ys, lanes), f32),
            pltpu.VMEM((blocks, tall, lanes), f32),
            pltpu.VMEM((blocks, ys, lanes), f32),
            pltpu.VMEM((ITERS, blocks, tall, lanes), f32),
            pltpu.VMEM((ITERS, blocks, tall, lanes), f32),
            pltpu.VMEM((rounds, 2, species * xs, lanes), f32),
            pltpu.VMEM((rounds, 2, species * xs, lanes), f32),
            pltpu.VMEM((rounds, ys, lanes), f32),
            pltpu.VMEM((rounds, 2, ys, lanes), f32),
            pltpu.VMEM((ITERS, 1, lanes), f32),
            pltpu.VMEM((ITERS, count, 1, lanes), f32),
            pltpu.SemaphoreType.DMA((rounds, 2)),
            pltpu.SemaphoreType.DMA((rounds, 2)),
            pltpu.SemaphoreType.DMA((rounds, 2)),
            pltpu.SemaphoreType.DMA((rounds, 2)),
            pltpu.SemaphoreType.DMA((ITERS,)),
            pltpu.SemaphoreType.DMA((ITERS,)),
            pltpu.SemaphoreType.DMA,
        ],
        compiler_params=pltpu.CompilerParams(collective_id=0, has_side_effects=True),
    )(state, member_set, *tables)


def solution(mesh):
    return jax.shard_map(
        functools.partial(shards, mesh.shape["gy"], mesh.shape["gz"]),
        mesh=mesh,
        in_specs=(P("ens", None, None, "gy", "gz"), P("ens"), P(), P(), P(), P()),
        out_specs=P("ens", None, None, "gy", "gz"),
        check_vma=False,
    )
```

```python
import functools

import jax
import jax.numpy as jnp
from jax import lax
from jax.experimental import pallas as pl
from jax.experimental.pallas import tpu as pltpu
from jax.sharding import PartitionSpec as P

ITERS = 4
TOP = 8


def kernel(
    ny, nz,
    state_ref, set_ref, courant_hbm, diffuse_hbm, react_hbm, quad_hbm,
    out_ref,
    courant_ref, diffuse_ref, react_ref, quad_ref, table_sem,
    cells, padded, further, images, basis,
    ysend, yrecv, zsend, zrecv, dsend, drecv,
    ysend_sem, yrecv_sem, zsend_sem, zrecv_sem, dsend_sem, drecv_sem, load_sem,
):
    species, xs, ys, lanes = cells.shape
    count = ny * nz
    gy, gz = lax.axis_index("gy"), lax.axis_index("gz")
    me = gy * nz + gz
    low, high = TOP - 1, TOP + ys
    halo_rounds = ITERS + 1

    load = pltpu.make_async_copy(state_ref.at[0], cells, load_sem)
    load.start()
    tables = [
        pltpu.make_async_copy(source, target, table_sem.at[n])
        for n, (source, target) in enumerate((
            (courant_hbm, courant_ref), (diffuse_hbm, diffuse_ref), (react_hbm, react_ref), (quad_hbm, quad_ref)))
    ]
    for table in tables:
        table.start()

    def peer(step):
        other = lax.rem(me + step, count)
        return {"gy": lax.div(other, nz), "gz": lax.rem(other, nz)}

    barrier = pltpu.get_barrier_semaphore()
    for step in range(1, count):
        pl.semaphore_signal(
            barrier, inc=1, device_id=peer(step), device_id_type=pl.DeviceIdType.MESH
        )

    slab = jnp.zeros((ys, lanes), jnp.float32)
    for k in range(species):
        for edge in (0, xs + 1):
            where = k * (xs + 2) + edge
            padded[where, TOP:high, :] = slab
            for j in range(ITERS - 1):
                images[j, where, TOP:high, :] = slab
            basis[0, where, TOP:high, :] = slab
    for side, outermost in ((0, gy == 0), (1, gy == ny - 1)):
        @pl.when(outermost)
        def _():
            for r in range(halo_rounds):
                yrecv[r, side] = jnp.zeros(yrecv.shape[2:], jnp.float32)
    for side, outermost in ((0, gz == 0), (1, gz == nz - 1)):
        @pl.when(outermost)
        def _():
            for r in range(halo_rounds):
                zrecv[r, side] = jnp.zeros(zrecv.shape[2:], jnp.float32)

    lane = lax.broadcasted_iota(jnp.int32, (ys, lanes), 1)
    odd = lax.rem(lane, 2) == 1
    first, last = lane == 0, lane == lanes - 1
    line_of = lax.broadcasted_iota(jnp.int32, (ys, lanes), 0)
    top, bottom = line_of == 0, line_of == ys - 1
    empty = jnp.zeros((1, lanes), jnp.float32)

    def halo_copies(r):
        listed = []
        for side, there, inside in ((0, 1, gy > 0), (1, 0, gy < ny - 1)):
            listed.append((inside, gy < ny - 1 if side == 0 else gy > 0,
                pltpu.make_async_remote_copy(
                    src_ref=ysend.at[r, side], dst_ref=yrecv.at[r, there],
                    send_sem=ysend_sem.at[r, side], recv_sem=yrecv_sem.at[r, there],
                    device_id={"gy": gy - 1 if side == 0 else gy + 1},
                    device_id_type=pl.DeviceIdType.MESH)))
        for side, there, inside in ((0, 1, gz > 0), (1, 0, gz < nz - 1)):
            listed.append((inside, gz < nz - 1 if side == 0 else gz > 0,
                pltpu.make_async_remote_copy(
                    src_ref=zsend.at[r], dst_ref=zrecv.at[r, there],
                    send_sem=zsend_sem.at[r, side], recv_sem=zrecv_sem.at[r, there],
                    device_id={"gz": gz - 1 if side == 0 else gz + 1},
                    device_id_type=pl.DeviceIdType.MESH)))
        return listed

    def start_halo(r):
        for inside, _, copy in halo_copies(r):
            @pl.when(inside)
            def _():
                copy.start()

    def finish_halo(r):
        for _, arriving, copy in halo_copies(r):
            @pl.when(arriving)
            def _():
                copy.wait_recv()
        return jnp.where(odd, zrecv[r, 0], pltpu.roll(zrecv[r, 1], lanes - 2, 1))

    def slot(k, x):
        return k * (xs + 2) + x + 1, k * xs + x

    def pack(zpack, block, r, k, x):
        _, j = slot(k, x)
        ysend[r, 0, pl.ds(j, 1), :] = block[0:1, :]
        ysend[r, 1, pl.ds(j, 1), :] = block[ys - 1 : ys, :]
        turned = pltpu.roll(block, 2 * j, 1)
        here = (lane == 2 * j) | (lane == lax.rem(2 * j + lanes - 1, lanes))
        return jnp.where(here, turned, zpack)

    def turned_back(zhalo, j):
        return pltpu.roll(zhalo, lax.rem(lanes + 1 - 2 * j + lanes, lanes), 1)

    def outer(r, zhalo, k, x, below, above, before, after):
        _, j = slot(k, x)
        edge = turned_back(zhalo, j)
        lines = jnp.where(
            top, yrecv[r, 0, pl.ds(j, 1), :] * below,
            jnp.where(bottom, yrecv[r, 1, pl.ds(j, 1), :] * above, 0.0))
        return lines + jnp.where(first, edge * before, jnp.where(last, edge * after, 0.0))

    def beside(ref, lead, zhalo, k, x):
        i, j = slot(k, x)
        at = lambda a, b: ref[lead + (a, slice(b, b + ys), slice(None))]
        here = at(i, TOP)
        edge = 0.0 if zhalo is None else turned_back(zhalo, j)
        before = jnp.where(first, edge, pltpu.roll(here, 1, 1))
        after = jnp.where(last, edge, pltpu.roll(here, lanes - 1, 1))
        return (here, (at(i - 1, TOP), at(i + 1, TOP)), (at(i, TOP - 1), at(i, TOP + 1)),
                (before, after))

    def fold(value):
        total = value[0:8]
        for row in range(8, ys, 8):
            total = total + value[row : row + 8]
        return total

    load.wait()

    def take(x, zpack):
        for k in range(species):
            block = cells[k, x]
            i = slot(k, x)[0]
            padded[i, TOP:high, :] = block
            padded[i, low : low + 1, :] = empty
            padded[i, high : high + 1, :] = empty
            zpack = pack(zpack, block, 0, k, x)
        return zpack

    zsend[0] = lax.fori_loop(0, xs, take, jnp.zeros((ys, lanes), jnp.float32), unroll=2)
    pl.semaphore_wait(barrier, count - 1)
    start_halo(0)

    for table in tables:
        table.wait()
    member = set_ref[0]
    courant = [courant_ref[d, member] for d in range(3)]
    strength = [diffuse_ref[k, member] for k in range(species)]
    rates = [[react_ref[k, l, member] for l in range(species)] for k in range(species)]
    coupling = [quad_ref[k, member] for k in range(species)]
    ahead = [jnp.maximum(c, 0.0) for c in courant]
    back = [jnp.minimum(c, 0.0) for c in courant]
    keep = 1.0
    for d in range(3):
        keep = keep - ahead[d] + back[d]

    def set_rows(ref, lead, r, k, x):
        i, j = slot(k, x)
        ref[lead + (i, slice(low, low + 1), slice(None))] = yrecv[r, 0, pl.ds(j, 1), :]
        ref[lead + (i, slice(high, high + 1), slice(None))] = yrecv[r, 1, pl.ds(j, 1), :]

    def explicit(x, carry):
        near = [beside(padded, (), None, k, x) for k in range(species)]
        a, b = near[0][0], near[1][0]
        coupled = a * b / (1.0 + a * a + b * b)
        for k in range(species):
            here = near[k][0]
            total = keep * here
            for d in range(3):
                total = total + ahead[d] * near[k][1 + d][0] - back[d] * near[k][1 + d][1]
            for l in range(species):
                total = total + rates[k][l] * near[l][0]
            i = slot(k, x)[0]
            basis[0, i, TOP:high, :] = total + coupling[k] * coupled
            basis[0, i, low : low + 1, :] = empty
            basis[0, i, high : high + 1, :] = empty
        return carry

    lax.fori_loop(0, xs, explicit, 0, unroll=2)
    zhalo0 = finish_halo(0)

    def explicit_outer(x, zpack):
        for k in range(species):
            i = slot(k, x)[0]
            total = basis[0, i, TOP:high, :] + outer(
                0, zhalo0, k, x, ahead[1], -back[1], ahead[2], -back[2])
            basis[0, i, TOP:high, :] = total
            zpack = pack(zpack, total, 1, k, x)
        return zpack

    zsend[1] = lax.fori_loop(
        0, xs, explicit_outer, jnp.zeros((ys, lanes), jnp.float32), unroll=2)
    start_halo(1)

    cosines, sines, triangle = [], [], []
    target = None

    def rotate(entries, column):
        for earlier in range(column):
            rotated = cosines[earlier] * entries[earlier] + sines[earlier] * entries[earlier + 1]
            entries[earlier + 1] = (
                cosines[earlier] * entries[earlier + 1] - sines[earlier] * entries[earlier]
            )
            entries[earlier] = rotated
        radius = jnp.sqrt(
            entries[column] * entries[column] + entries[column + 1] * entries[column + 1]
        )
        cosine, sine = entries[column] / radius, entries[column + 1] / radius
        cosines.append(cosine)
        sines.append(sine)
        triangle.append(entries[:column] + [radius])
        target.append(-sine * target[column])
        target[column] = cosine * target[column]

    zero = jnp.zeros((8, lanes), jnp.float32)
    blank = jnp.zeros((ys, lanes), jnp.float32)

    def applied(ref, lead, k, x, halo):
        here, nearx, neary, nearz = beside(ref, lead, halo, k, x)
        around = nearx[0] + nearx[1] + (neary[0] + neary[1]) + (nearz[0] + nearz[1])
        return here, (1.0 + 6.0 * strength[k]) * here - strength[k] * around

    def share(column, parts):
        mine = jnp.zeros((1, lanes), jnp.float32)
        for p, part in enumerate(parts):
            row = jnp.sum(part, axis=0, keepdims=True)
            mine = jnp.where(lane[0:1] == p, jnp.sum(row, axis=1, keepdims=True), mine)
        dsend[column] = mine
        for step in range(1, count):
            pltpu.make_async_remote_copy(
                src_ref=dsend.at[column], dst_ref=drecv.at[column, me],
                send_sem=dsend_sem.at[column], recv_sem=drecv_sem.at[column],
                device_id=peer(step), device_id_type=pl.DeviceIdType.MESH,
            ).start()
        drecv[column, me] = mine

    def gathered(column, products):
        others = drecv.at[column, pl.ds(0, count - 1)]
        pltpu.make_async_copy(others, others, drecv_sem.at[column]).wait()
        grid = drecv[column, 0]
        for other in range(1, count):
            grid = grid + drecv[column, other]
        return [grid[:, p : p + 1] for p in range(products)]

    def implicit(x, carry):
        for k in range(species):
            images[0, slot(k, x)[0], TOP:high, :] = applied(basis, (0,), k, x, None)[1]
        return carry

    lax.fori_loop(0, xs, implicit, 0, unroll=2)
    zhalo1 = finish_halo(1)

    def implicit_outer(x, carry):
        zpack, cross, square, own = carry
        for k in range(species):
            i = slot(k, x)[0]
            here = basis[0, i, TOP:high, :]
            lost = -strength[k]
            made = images[0, i, TOP:high, :] + outer(1, zhalo1, k, x, lost, lost, lost, lost)
            images[0, i, TOP:high, :] = made
            zpack = pack(zpack, made, 2, k, x)
            cross = cross + fold(here * made)
            square = square + fold(made * made)
            own = own + fold(here * here)
        return zpack, cross, square, own

    zpack, *parts = lax.fori_loop(0, xs, implicit_outer, (blank, zero, zero, zero), unroll=2)
    share(0, parts)
    zsend[2] = zpack
    start_halo(2)
    halos = [finish_halo(2)]

    def rows1(x, carry):
        for k in range(species):
            set_rows(images, (0,), 2, k, x)
        return carry

    lax.fori_loop(0, xs, rows1, 0, unroll=4)

    pending = None
    for column in range(ITERS):
        more = column + 1 < ITERS
        wider = column + 2 < ITERS
        r = column + 3
        if more:
            def again(x, zpack):
                for k in range(species):
                    _, made = applied(images, (column,), k, x, halos[column])
                    further[slot(k, x)[0]] = made
                    if wider:
                        zpack = pack(zpack, made, r, k, x)
                return zpack

            zpack = lax.fori_loop(0, xs, again, blank, unroll=2)
            if wider:
                zsend[r] = zpack
                start_halo(r)
        if pending is not None:
            rotate(*pending)
        sums = gathered(column, 3 if column == 0 else column + 2)
        if column == 0:
            beta = jnp.sqrt(sums[2])
            inverse_beta = 1.0 / beta
            target = [beta]
            square = inverse_beta * inverse_beta
            projections = [sums[0] * square]
            length_sq = sums[1] * square
        else:
            projections = [sums[0] * inverse_beta] + sums[1 : column + 1]
            length_sq = sums[column + 1]
        kept = projections[0] * projections[0]
        for value in projections[1:]:
            kept = kept + value * value
        norm_next = jnp.sqrt(length_sq - kept)
        pending = (projections + [norm_next], column)
        if not more:
            break
        inverse = 1.0 / norm_next
        gain = inverse if column else inverse * inverse_beta
        gains = [-(projections[0] * inverse) * inverse_beta] + [
            -(value * inverse) for value in projections[1:]
        ]
        wide = jnp.broadcast_to(gain, (ys, lanes))
        wides = [jnp.broadcast_to(g, (ys, lanes)) for g in gains]

        def combine(x, sums):
            sums = list(sums)
            for k in range(species):
                i = slot(k, x)[0]
                olds = [basis[earlier, i, TOP:high, :] for earlier in range(column + 1)]
                vector = images[column, i, TOP:high, :] * wide
                made = further[i] * wide
                for earlier in range(column + 1):
                    vector = vector + olds[earlier] * wides[earlier]
                    made = made + images[earlier, i, TOP:high, :] * wides[earlier]
                basis[column + 1, i, TOP:high, :] = vector
                images[column + 1, i, TOP:high, :] = made
                for p, left in enumerate(olds + [vector, made]):
                    sums[p] = sums[p] + fold(left * made)
            return tuple(sums)

        share(column + 1, lax.fori_loop(0, xs, combine, (zero,) * (column + 3), unroll=2))
        if wider:
            fresh = finish_halo(r) * gain
            for earlier in range(column + 1):
                fresh = fresh + halos[earlier] * gains[earlier]
            halos.append(fresh)

            def borders(x, carry):
                for k in range(species):
                    i, j = slot(k, x)
                    for side, row in ((0, low), (1, high)):
                        line = yrecv[r, side, pl.ds(j, 1), :] * wide[0:1]
                        for earlier in range(column + 1):
                            line = line + images[earlier, i, row : row + 1, :] * wides[earlier][0:1]
                        images[column + 1, i, row : row + 1, :] = line
                return carry

            lax.fori_loop(0, xs, borders, 0, unroll=2)

    rotate(*pending)
    coeffs = [None] * ITERS
    for column in reversed(range(ITERS)):
        running = target[column]
        for further in range(column + 1, ITERS):
            running = running - triangle[further][column] * coeffs[further]
        coeffs[column] = running / triangle[column][column]
    coeffs[0] = coeffs[0] * inverse_beta
    wides = [jnp.broadcast_to(c, (ys, lanes)) for c in coeffs]

    def finish(x, carry):
        for k in range(species):
            i = slot(k, x)[0]
            total = basis[0, i, TOP:high, :] * wides[0]
            for column in range(1, ITERS):
                total = total + basis[column, i, TOP:high, :] * wides[column]
            out_ref[0, k, x] = total
        return carry

    lax.fori_loop(0, xs, finish, 0, unroll=2)

    for r in range(halo_rounds):
        for inside, _, copy in halo_copies(r):
            @pl.when(inside)
            def _():
                copy.wait_send()
    for column in range(ITERS):
        others = drecv.at[column, pl.ds(0, count - 1)]
        pltpu.make_async_copy(others, others, dsend_sem.at[column]).wait()


def shards(ny, nz, state, member_set, courant, diffusion, reaction, quadratic):
    _, species, xs, ys, lanes = state.shape
    blocks, tall = species * (xs + 2), TOP + ys + 8
    rounds, count = ITERS + 1, ny * nz
    f32 = jnp.float32
    anywhere = pl.BlockSpec(memory_space=pl.ANY)
    tables = (courant.T, diffusion.T, jnp.transpose(reaction, (1, 2, 0)), quadratic.T)
    return pl.pallas_call(
        functools.partial(kernel, ny, nz),
        out_shape=pltpu.VMEM(state.shape, f32),
        in_specs=[anywhere, pl.BlockSpec(memory_space=pltpu.SMEM)] + [anywhere] * len(tables),
        out_specs=pl.BlockSpec(memory_space=pltpu.VMEM),
        scratch_shapes=[pltpu.SMEM(table.shape, table.dtype) for table in tables] + [
            pltpu.SemaphoreType.DMA((len(tables),)),
            pltpu.VMEM((species, xs, ys, lanes), f32),
            pltpu.VMEM((blocks, tall, lanes), f32),
            pltpu.VMEM((blocks, ys, lanes), f32),
            pltpu.VMEM((ITERS, blocks, tall, lanes), f32),
            pltpu.VMEM((ITERS, blocks, tall, lanes), f32),
            pltpu.VMEM((rounds, 2, species * xs, lanes), f32),
            pltpu.VMEM((rounds, 2, species * xs, lanes), f32),
            pltpu.VMEM((rounds, ys, lanes), f32),
            pltpu.VMEM((rounds, 2, ys, lanes), f32),
            pltpu.VMEM((ITERS, 1, lanes), f32),
            pltpu.VMEM((ITERS, count, 1, lanes), f32),
            pltpu.SemaphoreType.DMA((rounds, 2)),
            pltpu.SemaphoreType.DMA((rounds, 2)),
            pltpu.SemaphoreType.DMA((rounds, 2)),
            pltpu.SemaphoreType.DMA((rounds, 2)),
            pltpu.SemaphoreType.DMA((ITERS,)),
            pltpu.SemaphoreType.DMA((ITERS,)),
            pltpu.SemaphoreType.DMA,
        ],
        compiler_params=pltpu.CompilerParams(collective_id=0, has_side_effects=True),
    )(state, member_set, *tables)


def solution(mesh):
    return jax.shard_map(
        functools.partial(shards, mesh.shape["gy"], mesh.shape["gz"]),
        mesh=mesh,
        in_specs=(P("ens", None, None, "gy", "gz"), P("ens"), P(), P(), P(), P()),
        out_specs=P("ens", None, None, "gy", "gz"),
        check_vma=False,
    )
```

```python
import functools

import jax
import jax.numpy as jnp
from jax import lax
from jax.experimental import pallas as pl
from jax.experimental.pallas import tpu as pltpu
from jax.sharding import PartitionSpec as P

ITERS = 4
TOP = 8


def kernel(
    ny, nz,
    state_ref, set_ref, courant_hbm, diffuse_hbm, react_hbm, quad_hbm,
    out_ref,
    courant_ref, diffuse_ref, react_ref, quad_ref, table_sem,
    cells, padded, further, images, basis,
    ysend, yrecv, zsend, zrecv, dsend, drecv,
    ysend_sem, yrecv_sem, zsend_sem, zrecv_sem, dsend_sem, drecv_sem, load_sem,
):
    species, xs, ys, lanes = cells.shape
    count = ny * nz
    gy, gz = lax.axis_index("gy"), lax.axis_index("gz")
    me = gy * nz + gz
    low, high = TOP - 1, TOP + ys
    halo_rounds = ITERS + 1

    load = pltpu.make_async_copy(state_ref.at[0], cells, load_sem)
    load.start()
    tables = [
        pltpu.make_async_copy(source, target, table_sem.at[n])
        for n, (source, target) in enumerate((
            (courant_hbm, courant_ref), (diffuse_hbm, diffuse_ref), (react_hbm, react_ref), (quad_hbm, quad_ref)))
    ]
    for table in tables:
        table.start()

    def turns(position, size):
        return [jnp.where(position + n >= size, position + n - size, position + n)
                for n in range(size)]

    around_y, around_z = turns(gy, ny), turns(gz, nz)

    def peer(step):
        return {"gy": around_y[step // nz], "gz": around_z[step % nz]}

    barrier = pltpu.get_barrier_semaphore()
    for step in range(1, count):
        pl.semaphore_signal(
            barrier, inc=1, device_id=peer(step), device_id_type=pl.DeviceIdType.MESH
        )

    slab = jnp.zeros((ys, lanes), jnp.float32)
    for k in range(species):
        for edge in (0, xs + 1):
            where = k * (xs + 2) + edge
            padded[where, TOP:high, :] = slab
            for j in range(ITERS - 1):
                images[j, where, TOP:high, :] = slab
            basis[0, where, TOP:high, :] = slab
    for side, outermost in ((0, gy == 0), (1, gy == ny - 1)):
        @pl.when(outermost)
        def _():
            for r in range(halo_rounds):
                yrecv[r, side] = jnp.zeros(yrecv.shape[2:], jnp.float32)
    for side, outermost in ((0, gz == 0), (1, gz == nz - 1)):
        @pl.when(outermost)
        def _():
            for r in range(halo_rounds):
                zrecv[r, side] = jnp.zeros(zrecv.shape[2:], jnp.float32)

    lane = lax.broadcasted_iota(jnp.int32, (ys, lanes), 1)
    odd = lax.rem(lane, 2) == 1
    first, last = lane == 0, lane == lanes - 1
    line_of = lax.broadcasted_iota(jnp.int32, (ys, lanes), 0)
    top, bottom = line_of == 0, line_of == ys - 1
    empty = jnp.zeros((1, lanes), jnp.float32)

    def halo_copies(r):
        listed = []
        for side, there, inside in ((0, 1, gy > 0), (1, 0, gy < ny - 1)):
            listed.append((inside, gy < ny - 1 if side == 0 else gy > 0,
                pltpu.make_async_remote_copy(
                    src_ref=ysend.at[r, side], dst_ref=yrecv.at[r, there],
                    send_sem=ysend_sem.at[r, side], recv_sem=yrecv_sem.at[r, there],
                    device_id={"gy": gy - 1 if side == 0 else gy + 1},
                    device_id_type=pl.DeviceIdType.MESH)))
        for side, there, inside in ((0, 1, gz > 0), (1, 0, gz < nz - 1)):
            listed.append((inside, gz < nz - 1 if side == 0 else gz > 0,
                pltpu.make_async_remote_copy(
                    src_ref=zsend.at[r], dst_ref=zrecv.at[r, there],
                    send_sem=zsend_sem.at[r, side], recv_sem=zrecv_sem.at[r, there],
                    device_id={"gz": gz - 1 if side == 0 else gz + 1},
                    device_id_type=pl.DeviceIdType.MESH)))
        return listed

    def start_halo(r):
        for inside, _, copy in halo_copies(r):
            @pl.when(inside)
            def _():
                copy.start()

    def finish_halo(r):
        for _, arriving, copy in halo_copies(r):
            @pl.when(arriving)
            def _():
                copy.wait_recv()
        return jnp.where(odd, zrecv[r, 0], pltpu.roll(zrecv[r, 1], lanes - 2, 1))

    def slot(k, x):
        return k * (xs + 2) + x + 1, k * xs + x

    def pack(zpack, block, r, k, x):
        _, j = slot(k, x)
        ysend[r, 0, pl.ds(j, 1), :] = block[0:1, :]
        ysend[r, 1, pl.ds(j, 1), :] = block[ys - 1 : ys, :]
        turned = pltpu.roll(block, 2 * j, 1)
        here = (lane == 2 * j) | (lane == lax.rem(2 * j + lanes - 1, lanes))
        return jnp.where(here, turned, zpack)

    def turned_back(zhalo, j):
        return pltpu.roll(zhalo, lax.rem(lanes + 1 - 2 * j + lanes, lanes), 1)

    def outer(r, zhalo, k, x, below, above, before, after):
        _, j = slot(k, x)
        edge = turned_back(zhalo, j)
        lines = jnp.where(
            top, yrecv[r, 0, pl.ds(j, 1), :] * below,
            jnp.where(bottom, yrecv[r, 1, pl.ds(j, 1), :] * above, 0.0))
        return lines + jnp.where(first, edge * before, jnp.where(last, edge * after, 0.0))

    def beside(ref, lead, zhalo, k, x):
        i, j = slot(k, x)
        at = lambda a, b: ref[lead + (a, slice(b, b + ys), slice(None))]
        here = at(i, TOP)
        edge = 0.0 if zhalo is None else turned_back(zhalo, j)
        before = jnp.where(first, edge, pltpu.roll(here, 1, 1))
        after = jnp.where(last, edge, pltpu.roll(here, lanes - 1, 1))
        return (here, (at(i - 1, TOP), at(i + 1, TOP)), (at(i, TOP - 1), at(i, TOP + 1)),
                (before, after))

    def fold(value):
        total = value[0:8]
        for row in range(8, ys, 8):
            total = total + value[row : row + 8]
        return total

    load.wait()

    def take(x, zpack):
        for k in range(species):
            block = cells[k, x]
            i = slot(k, x)[0]
            padded[i, TOP:high, :] = block
            padded[i, low : low + 1, :] = empty
            padded[i, high : high + 1, :] = empty
            zpack = pack(zpack, block, 0, k, x)
        return zpack

    zsend[0] = lax.fori_loop(0, xs, take, jnp.zeros((ys, lanes), jnp.float32), unroll=2)
    pl.semaphore_wait(barrier, count - 1)
    start_halo(0)

    for table in tables:
        table.wait()
    member = set_ref[0]
    courant = [courant_ref[d, member] for d in range(3)]
    strength = [diffuse_ref[k, member] for k in range(species)]
    rates = [[react_ref[k, l, member] for l in range(species)] for k in range(species)]
    coupling = [quad_ref[k, member] for k in range(species)]
    ahead = [jnp.maximum(c, 0.0) for c in courant]
    back = [jnp.minimum(c, 0.0) for c in courant]
    keep = 1.0
    for d in range(3):
        keep = keep - ahead[d] + back[d]

    def set_rows(ref, lead, r, k, x):
        i, j = slot(k, x)
        ref[lead + (i, slice(low, low + 1), slice(None))] = yrecv[r, 0, pl.ds(j, 1), :]
        ref[lead + (i, slice(high, high + 1), slice(None))] = yrecv[r, 1, pl.ds(j, 1), :]

    def explicit(x, carry):
        near = [beside(padded, (), None, k, x) for k in range(species)]
        a, b = near[0][0], near[1][0]
        coupled = a * b / (1.0 + a * a + b * b)
        for k in range(species):
            here = near[k][0]
            total = keep * here
            for d in range(3):
                total = total + ahead[d] * near[k][1 + d][0] - back[d] * near[k][1 + d][1]
            for l in range(species):
                total = total + rates[k][l] * near[l][0]
            i = slot(k, x)[0]
            basis[0, i, TOP:high, :] = total + coupling[k] * coupled
            basis[0, i, low : low + 1, :] = empty
            basis[0, i, high : high + 1, :] = empty
        return carry

    lax.fori_loop(0, xs, explicit, 0, unroll=2)
    zhalo0 = finish_halo(0)

    def explicit_outer(x, zpack):
        for k in range(species):
            i = slot(k, x)[0]
            total = basis[0, i, TOP:high, :] + outer(
                0, zhalo0, k, x, ahead[1], -back[1], ahead[2], -back[2])
            basis[0, i, TOP:high, :] = total
            zpack = pack(zpack, total, 1, k, x)
        return zpack

    zsend[1] = lax.fori_loop(
        0, xs, explicit_outer, jnp.zeros((ys, lanes), jnp.float32), unroll=2)
    start_halo(1)

    cosines, sines, triangle = [], [], []
    target = None

    def rotate(entries, column):
        for earlier in range(column):
            rotated = cosines[earlier] * entries[earlier] + sines[earlier] * entries[earlier + 1]
            entries[earlier + 1] = (
                cosines[earlier] * entries[earlier + 1] - sines[earlier] * entries[earlier]
            )
            entries[earlier] = rotated
        radius = jnp.sqrt(
            entries[column] * entries[column] + entries[column + 1] * entries[column + 1]
        )
        scale = 1.0 / radius
        cosine, sine = entries[column] * scale, entries[column + 1] * scale
        cosines.append(cosine)
        sines.append(sine)
        triangle.append(entries[:column] + [scale])
        target.append(-sine * target[column])
        target[column] = cosine * target[column]

    zero = jnp.zeros((8, lanes), jnp.float32)
    blank = jnp.zeros((ys, lanes), jnp.float32)

    def applied(ref, lead, k, x, halo):
        here, nearx, neary, nearz = beside(ref, lead, halo, k, x)
        around = nearx[0] + nearx[1] + (neary[0] + neary[1]) + (nearz[0] + nearz[1])
        return here, (1.0 + 6.0 * strength[k]) * here - strength[k] * around

    def share(column, parts):
        mine = jnp.zeros((1, lanes), jnp.float32)
        for p, part in enumerate(parts):
            row = jnp.sum(part, axis=0, keepdims=True)
            mine = jnp.where(lane[0:1] == p, jnp.sum(row, axis=1, keepdims=True), mine)
        dsend[column] = mine
        for step in range(1, count):
            pltpu.make_async_remote_copy(
                src_ref=dsend.at[column], dst_ref=drecv.at[column, me],
                send_sem=dsend_sem.at[column], recv_sem=drecv_sem.at[column],
                device_id=peer(step), device_id_type=pl.DeviceIdType.MESH,
            ).start()
        drecv[column, me] = mine

    def gathered(column, products):
        others = drecv.at[column, pl.ds(0, count - 1)]
        pltpu.make_async_copy(others, others, drecv_sem.at[column]).wait()
        grid = drecv[column, 0]
        for other in range(1, count):
            grid = grid + drecv[column, other]
        return [grid[:, p : p + 1] for p in range(products)]

    def implicit(x, carry):
        for k in range(species):
            images[0, slot(k, x)[0], TOP:high, :] = applied(basis, (0,), k, x, None)[1]
        return carry

    lax.fori_loop(0, xs, implicit, 0, unroll=2)
    zhalo1 = finish_halo(1)

    def implicit_outer(x, carry):
        zpack, cross, square, own = carry
        for k in range(species):
            i = slot(k, x)[0]
            here = basis[0, i, TOP:high, :]
            lost = -strength[k]
            made = images[0, i, TOP:high, :] + outer(1, zhalo1, k, x, lost, lost, lost, lost)
            images[0, i, TOP:high, :] = made
            zpack = pack(zpack, made, 2, k, x)
            cross = cross + fold(here * made)
            square = square + fold(made * made)
            own = own + fold(here * here)
        return zpack, cross, square, own

    zpack, *parts = lax.fori_loop(0, xs, implicit_outer, (blank, zero, zero, zero), unroll=2)
    share(0, parts)
    zsend[2] = zpack
    start_halo(2)
    halos = [finish_halo(2)]

    def rows1(x, carry):
        for k in range(species):
            set_rows(images, (0,), 2, k, x)
        return carry

    lax.fori_loop(0, xs, rows1, 0, unroll=4)

    pending = None
    for column in range(ITERS):
        more = column + 1 < ITERS
        wider = column + 2 < ITERS
        r = column + 3
        if more:
            def again(x, zpack):
                for k in range(species):
                    _, made = applied(images, (column,), k, x, halos[column])
                    further[slot(k, x)[0]] = made
                    if wider:
                        zpack = pack(zpack, made, r, k, x)
                return zpack

            zpack = lax.fori_loop(0, xs, again, blank, unroll=2)
            if wider:
                zsend[r] = zpack
                start_halo(r)
        if pending is not None:
            rotate(*pending)
        sums = gathered(column, 3 if column == 0 else column + 2)
        if column == 0:
            beta = jnp.sqrt(sums[2])
            inverse_beta = 1.0 / beta
            target = [beta]
            square = inverse_beta * inverse_beta
            projections = [sums[0] * square]
            length_sq = sums[1] * square
        else:
            projections = [sums[0] * inverse_beta] + sums[1 : column + 1]
            length_sq = sums[column + 1]
        kept = projections[0] * projections[0]
        for value in projections[1:]:
            kept = kept + value * value
        norm_next = jnp.sqrt(length_sq - kept)
        pending = (projections + [norm_next], column)
        if not more:
            break
        inverse = 1.0 / norm_next
        gain = inverse if column else inverse * inverse_beta
        gains = [-(projections[0] * inverse) * inverse_beta] + [
            -(value * inverse) for value in projections[1:]
        ]
        wide = jnp.broadcast_to(gain, (ys, lanes))
        wides = [jnp.broadcast_to(g, (ys, lanes)) for g in gains]

        def combine(x, sums):
            sums = list(sums)
            for k in range(species):
                i = slot(k, x)[0]
                olds = [basis[earlier, i, TOP:high, :] for earlier in range(column + 1)]
                vector = images[column, i, TOP:high, :] * wide
                made = further[i] * wide
                for earlier in range(column + 1):
                    vector = vector + olds[earlier] * wides[earlier]
                    made = made + images[earlier, i, TOP:high, :] * wides[earlier]
                basis[column + 1, i, TOP:high, :] = vector
                images[column + 1, i, TOP:high, :] = made
                for p, left in enumerate(olds + [vector, made]):
                    sums[p] = sums[p] + fold(left * made)
            return tuple(sums)

        share(column + 1, lax.fori_loop(0, xs, combine, (zero,) * (column + 3), unroll=2))
        if wider:
            fresh = finish_halo(r) * gain
            for earlier in range(column + 1):
                fresh = fresh + halos[earlier] * gains[earlier]
            halos.append(fresh)

            def borders(x, carry):
                for k in range(species):
                    i, j = slot(k, x)
                    for side, row in ((0, low), (1, high)):
                        line = yrecv[r, side, pl.ds(j, 1), :] * wide[0:1]
                        for earlier in range(column + 1):
                            line = line + images[earlier, i, row : row + 1, :] * wides[earlier][0:1]
                        images[column + 1, i, row : row + 1, :] = line
                return carry

            lax.fori_loop(0, xs, borders, 0, unroll=2)

    rotate(*pending)
    coeffs = [None] * ITERS
    for column in reversed(range(ITERS)):
        running = target[column]
        for further in range(column + 1, ITERS):
            running = running - triangle[further][column] * coeffs[further]
        coeffs[column] = running * triangle[column][column]
    coeffs[0] = coeffs[0] * inverse_beta
    wides = [jnp.broadcast_to(c, (ys, lanes)) for c in coeffs]

    def finish(x, carry):
        for k in range(species):
            i = slot(k, x)[0]
            total = basis[0, i, TOP:high, :] * wides[0]
            for column in range(1, ITERS):
                total = total + basis[column, i, TOP:high, :] * wides[column]
            out_ref[0, k, x] = total
        return carry

    lax.fori_loop(0, xs, finish, 0, unroll=2)

    for r in range(halo_rounds):
        for inside, _, copy in halo_copies(r):
            @pl.when(inside)
            def _():
                copy.wait_send()
    for column in range(ITERS):
        others = drecv.at[column, pl.ds(0, count - 1)]
        pltpu.make_async_copy(others, others, dsend_sem.at[column]).wait()


def shards(ny, nz, state, member_set, courant, diffusion, reaction, quadratic):
    _, species, xs, ys, lanes = state.shape
    blocks, tall = species * (xs + 2), TOP + ys + 8
    rounds, count = ITERS + 1, ny * nz
    f32 = jnp.float32
    anywhere = pl.BlockSpec(memory_space=pl.ANY)
    tables = (courant.T, diffusion.T, jnp.transpose(reaction, (1, 2, 0)), quadratic.T)
    return pl.pallas_call(
        functools.partial(kernel, ny, nz),
        out_shape=pltpu.VMEM(state.shape, f32),
        in_specs=[anywhere, pl.BlockSpec(memory_space=pltpu.SMEM)] + [anywhere] * len(tables),
        out_specs=pl.BlockSpec(memory_space=pltpu.VMEM),
        scratch_shapes=[pltpu.SMEM(table.shape, table.dtype) for table in tables] + [
            pltpu.SemaphoreType.DMA((len(tables),)),
            pltpu.VMEM((species, xs, ys, lanes), f32),
            pltpu.VMEM((blocks, tall, lanes), f32),
            pltpu.VMEM((blocks, ys, lanes), f32),
            pltpu.VMEM((ITERS, blocks, tall, lanes), f32),
            pltpu.VMEM((ITERS, blocks, tall, lanes), f32),
            pltpu.VMEM((rounds, 2, species * xs, lanes), f32),
            pltpu.VMEM((rounds, 2, species * xs, lanes), f32),
            pltpu.VMEM((rounds, ys, lanes), f32),
            pltpu.VMEM((rounds, 2, ys, lanes), f32),
            pltpu.VMEM((ITERS, 1, lanes), f32),
            pltpu.VMEM((ITERS, count, 1, lanes), f32),
            pltpu.SemaphoreType.DMA((rounds, 2)),
            pltpu.SemaphoreType.DMA((rounds, 2)),
            pltpu.SemaphoreType.DMA((rounds, 2)),
            pltpu.SemaphoreType.DMA((rounds, 2)),
            pltpu.SemaphoreType.DMA((ITERS,)),
            pltpu.SemaphoreType.DMA((ITERS,)),
            pltpu.SemaphoreType.DMA,
        ],
        compiler_params=pltpu.CompilerParams(collective_id=0, has_side_effects=True),
    )(state, member_set, *tables)


def solution(mesh):
    return jax.shard_map(
        functools.partial(shards, mesh.shape["gy"], mesh.shape["gz"]),
        mesh=mesh,
        in_specs=(P("ens", None, None, "gy", "gz"), P("ens"), P(), P(), P(), P()),
        out_specs=P("ens", None, None, "gy", "gz"),
        check_vma=False,
    )
```

```python
import functools

import jax
import jax.numpy as jnp
from jax import lax
from jax.experimental import pallas as pl
from jax.experimental.pallas import tpu as pltpu
from jax.sharding import PartitionSpec as P

ITERS = 4
TOP = 8


def kernel(
    ny, nz,
    state_ref, set_ref, courant_hbm, diffuse_hbm, react_hbm, quad_hbm,
    out_ref,
    courant_ref, diffuse_ref, react_ref, quad_ref, table_sem,
    cells, padded, further, images, basis,
    ysend, yrecv, zsend, zrecv, dsend, drecv,
    ysend_sem, yrecv_sem, zsend_sem, zrecv_sem, dsend_sem, drecv_sem, load_sem,
):
    species, xs, ys, lanes = cells.shape
    count = ny * nz
    gy, gz = lax.axis_index("gy"), lax.axis_index("gz")
    me = gy * nz + gz
    low, high = TOP - 1, TOP + ys
    halo_rounds = ITERS + 1

    pieces = load_sem.shape[0]
    width = xs // pieces
    loads = []
    for n in range(pieces):
        part = (slice(None), pl.ds(n * width, width))
        loads.append(
            pltpu.make_async_copy(state_ref.at[(0,) + part], cells.at[part], load_sem.at[n]))
        loads[n].start()
    tables = [
        pltpu.make_async_copy(source, target, table_sem.at[n])
        for n, (source, target) in enumerate((
            (courant_hbm, courant_ref), (diffuse_hbm, diffuse_ref), (react_hbm, react_ref), (quad_hbm, quad_ref)))
    ]
    for table in tables:
        table.start()

    def turns(position, size):
        return [jnp.where(position + n >= size, position + n - size, position + n)
                for n in range(size)]

    around_y, around_z = turns(gy, ny), turns(gz, nz)

    def peer(step):
        return {"gy": around_y[step // nz], "gz": around_z[step % nz]}

    barrier = pltpu.get_barrier_semaphore()
    for step in range(1, count):
        pl.semaphore_signal(
            barrier, inc=1, device_id=peer(step), device_id_type=pl.DeviceIdType.MESH
        )

    slab = jnp.zeros((ys, lanes), jnp.float32)
    for k in range(species):
        for edge in (0, xs + 1):
            where = k * (xs + 2) + edge
            padded[where, TOP:high, :] = slab
            for j in range(ITERS - 1):
                images[j, where, TOP:high, :] = slab
            basis[0, where, TOP:high, :] = slab
    for side, outermost in ((0, gy == 0), (1, gy == ny - 1)):
        @pl.when(outermost)
        def _():
            for r in range(halo_rounds):
                yrecv[r, side] = jnp.zeros(yrecv.shape[2:], jnp.float32)
    for side, outermost in ((0, gz == 0), (1, gz == nz - 1)):
        @pl.when(outermost)
        def _():
            for r in range(halo_rounds):
                zrecv[r, side] = jnp.zeros(zrecv.shape[2:], jnp.float32)

    lane = lax.broadcasted_iota(jnp.int32, (ys, lanes), 1)
    odd = lax.rem(lane, 2) == 1
    first, last = lane == 0, lane == lanes - 1
    line_of = lax.broadcasted_iota(jnp.int32, (ys, lanes), 0)
    top, bottom = line_of == 0, line_of == ys - 1
    empty = jnp.zeros((1, lanes), jnp.float32)

    def halo_copies(r):
        listed = []
        for side, there, inside in ((0, 1, gy > 0), (1, 0, gy < ny - 1)):
            listed.append((inside, gy < ny - 1 if side == 0 else gy > 0,
                pltpu.make_async_remote_copy(
                    src_ref=ysend.at[r, side], dst_ref=yrecv.at[r, there],
                    send_sem=ysend_sem.at[r, side], recv_sem=yrecv_sem.at[r, there],
                    device_id={"gy": gy - 1 if side == 0 else gy + 1},
                    device_id_type=pl.DeviceIdType.MESH)))
        for side, there, inside in ((0, 1, gz > 0), (1, 0, gz < nz - 1)):
            listed.append((inside, gz < nz - 1 if side == 0 else gz > 0,
                pltpu.make_async_remote_copy(
                    src_ref=zsend.at[r], dst_ref=zrecv.at[r, there],
                    send_sem=zsend_sem.at[r, side], recv_sem=zrecv_sem.at[r, there],
                    device_id={"gz": gz - 1 if side == 0 else gz + 1},
                    device_id_type=pl.DeviceIdType.MESH)))
        return listed

    def start_halo(r):
        for inside, _, copy in halo_copies(r):
            @pl.when(inside)
            def _():
                copy.start()

    def finish_halo(r):
        for _, arriving, copy in halo_copies(r):
            @pl.when(arriving)
            def _():
                copy.wait_recv()
        return jnp.where(odd, zrecv[r, 0], pltpu.roll(zrecv[r, 1], lanes - 2, 1))

    def slot(k, x):
        return k * (xs + 2) + x + 1, k * xs + x

    def pack(zpack, block, r, k, x):
        _, j = slot(k, x)
        ysend[r, 0, pl.ds(j, 1), :] = block[0:1, :]
        ysend[r, 1, pl.ds(j, 1), :] = block[ys - 1 : ys, :]
        turned = pltpu.roll(block, 2 * j, 1)
        here = (lane == 2 * j) | (lane == lax.rem(2 * j + lanes - 1, lanes))
        return jnp.where(here, turned, zpack)

    def turned_back(zhalo, j):
        return pltpu.roll(zhalo, lax.rem(lanes + 1 - 2 * j + lanes, lanes), 1)

    def outer(r, zhalo, k, x, below, above, before, after):
        _, j = slot(k, x)
        edge = turned_back(zhalo, j)
        lines = jnp.where(
            top, yrecv[r, 0, pl.ds(j, 1), :] * below,
            jnp.where(bottom, yrecv[r, 1, pl.ds(j, 1), :] * above, 0.0))
        return lines + jnp.where(first, edge * before, jnp.where(last, edge * after, 0.0))

    def beside(ref, lead, zhalo, k, x):
        i, j = slot(k, x)
        at = lambda a, b: ref[lead + (a, slice(b, b + ys), slice(None))]
        here = at(i, TOP)
        edge = 0.0 if zhalo is None else turned_back(zhalo, j)
        before = jnp.where(first, edge, pltpu.roll(here, 1, 1))
        after = jnp.where(last, edge, pltpu.roll(here, lanes - 1, 1))
        return (here, (at(i - 1, TOP), at(i + 1, TOP)), (at(i, TOP - 1), at(i, TOP + 1)),
                (before, after))

    def fold(value):
        total = value[0:8]
        for row in range(8, ys, 8):
            total = total + value[row : row + 8]
        return total

    def take(x, zpack):
        for k in range(species):
            block = cells[k, x]
            i = slot(k, x)[0]
            padded[i, TOP:high, :] = block
            padded[i, low : low + 1, :] = empty
            padded[i, high : high + 1, :] = empty
            zpack = pack(zpack, block, 0, k, x)
        return zpack

    zpack = jnp.zeros((ys, lanes), jnp.float32)
    for n in range(pieces):
        loads[n].wait()
        zpack = lax.fori_loop(n * width, (n + 1) * width, take, zpack, unroll=2)
    zsend[0] = zpack
    pl.semaphore_wait(barrier, count - 1)
    start_halo(0)

    for table in tables:
        table.wait()
    member = set_ref[0]
    courant = [courant_ref[d, member] for d in range(3)]
    strength = [diffuse_ref[k, member] for k in range(species)]
    rates = [[react_ref[k, l, member] for l in range(species)] for k in range(species)]
    coupling = [quad_ref[k, member] for k in range(species)]
    ahead = [jnp.maximum(c, 0.0) for c in courant]
    back = [jnp.minimum(c, 0.0) for c in courant]
    keep = 1.0
    for d in range(3):
        keep = keep - ahead[d] + back[d]

    def set_rows(ref, lead, r, k, x):
        i, j = slot(k, x)
        ref[lead + (i, slice(low, low + 1), slice(None))] = yrecv[r, 0, pl.ds(j, 1), :]
        ref[lead + (i, slice(high, high + 1), slice(None))] = yrecv[r, 1, pl.ds(j, 1), :]

    def explicit(x, carry):
        near = [beside(padded, (), None, k, x) for k in range(species)]
        a, b = near[0][0], near[1][0]
        coupled = a * b / (1.0 + a * a + b * b)
        for k in range(species):
            here = near[k][0]
            total = keep * here
            for d in range(3):
                total = total + ahead[d] * near[k][1 + d][0] - back[d] * near[k][1 + d][1]
            for l in range(species):
                total = total + rates[k][l] * near[l][0]
            i = slot(k, x)[0]
            basis[0, i, TOP:high, :] = total + coupling[k] * coupled
            basis[0, i, low : low + 1, :] = empty
            basis[0, i, high : high + 1, :] = empty
        return carry

    lax.fori_loop(0, xs, explicit, 0, unroll=2)
    zhalo0 = finish_halo(0)

    def explicit_outer(x, zpack):
        for k in range(species):
            i = slot(k, x)[0]
            total = basis[0, i, TOP:high, :] + outer(
                0, zhalo0, k, x, ahead[1], -back[1], ahead[2], -back[2])
            basis[0, i, TOP:high, :] = total
            zpack = pack(zpack, total, 1, k, x)
        return zpack

    zsend[1] = lax.fori_loop(
        0, xs, explicit_outer, jnp.zeros((ys, lanes), jnp.float32), unroll=2)
    start_halo(1)

    cosines, sines, triangle = [], [], []
    target = None

    def rotate(entries, column):
        for earlier in range(column):
            rotated = cosines[earlier] * entries[earlier] + sines[earlier] * entries[earlier + 1]
            entries[earlier + 1] = (
                cosines[earlier] * entries[earlier + 1] - sines[earlier] * entries[earlier]
            )
            entries[earlier] = rotated
        radius = jnp.sqrt(
            entries[column] * entries[column] + entries[column + 1] * entries[column + 1]
        )
        scale = 1.0 / radius
        cosine, sine = entries[column] * scale, entries[column + 1] * scale
        cosines.append(cosine)
        sines.append(sine)
        triangle.append(entries[:column] + [scale])
        target.append(-sine * target[column])
        target[column] = cosine * target[column]

    zero = jnp.zeros((8, lanes), jnp.float32)
    blank = jnp.zeros((ys, lanes), jnp.float32)

    def applied(ref, lead, k, x, halo):
        here, nearx, neary, nearz = beside(ref, lead, halo, k, x)
        around = nearx[0] + nearx[1] + (neary[0] + neary[1]) + (nearz[0] + nearz[1])
        return here, (1.0 + 6.0 * strength[k]) * here - strength[k] * around

    def share(column, parts):
        mine = jnp.zeros((1, lanes), jnp.float32)
        for p, part in enumerate(parts):
            row = jnp.sum(part, axis=0, keepdims=True)
            mine = jnp.where(lane[0:1] == p, jnp.sum(row, axis=1, keepdims=True), mine)
        dsend[column] = mine
        for step in range(1, count):
            pltpu.make_async_remote_copy(
                src_ref=dsend.at[column], dst_ref=drecv.at[column, me],
                send_sem=dsend_sem.at[column], recv_sem=drecv_sem.at[column],
                device_id=peer(step), device_id_type=pl.DeviceIdType.MESH,
            ).start()
        drecv[column, me] = mine

    def gathered(column, products):
        others = drecv.at[column, pl.ds(0, count - 1)]
        pltpu.make_async_copy(others, others, drecv_sem.at[column]).wait()
        grid = drecv[column, 0]
        for other in range(1, count):
            grid = grid + drecv[column, other]
        return [grid[:, p : p + 1] for p in range(products)]

    def implicit(x, carry):
        for k in range(species):
            images[0, slot(k, x)[0], TOP:high, :] = applied(basis, (0,), k, x, None)[1]
        return carry

    lax.fori_loop(0, xs, implicit, 0, unroll=2)
    zhalo1 = finish_halo(1)

    def implicit_outer(x, carry):
        zpack, cross, square, own = carry
        for k in range(species):
            i = slot(k, x)[0]
            here = basis[0, i, TOP:high, :]
            lost = -strength[k]
            made = images[0, i, TOP:high, :] + outer(1, zhalo1, k, x, lost, lost, lost, lost)
            images[0, i, TOP:high, :] = made
            zpack = pack(zpack, made, 2, k, x)
            cross = cross + fold(here * made)
            square = square + fold(made * made)
            own = own + fold(here * here)
        return zpack, cross, square, own

    zpack, *parts = lax.fori_loop(0, xs, implicit_outer, (blank, zero, zero, zero), unroll=2)
    share(0, parts)
    zsend[2] = zpack
    start_halo(2)
    halos = [finish_halo(2)]

    def rows1(x, carry):
        for k in range(species):
            set_rows(images, (0,), 2, k, x)
        return carry

    lax.fori_loop(0, xs, rows1, 0, unroll=4)

    pending = None
    for column in range(ITERS):
        more = column + 1 < ITERS
        wider = column + 2 < ITERS
        r = column + 3
        if more:
            def again(x, zpack):
                for k in range(species):
                    _, made = applied(images, (column,), k, x, halos[column])
                    further[slot(k, x)[0]] = made
                    if wider:
                        zpack = pack(zpack, made, r, k, x)
                return zpack

            zpack = lax.fori_loop(0, xs, again, blank, unroll=2)
            if wider:
                zsend[r] = zpack
                start_halo(r)
        if pending is not None:
            rotate(*pending)
        sums = gathered(column, 3 if column == 0 else column + 2)
        if column == 0:
            beta = jnp.sqrt(sums[2])
            inverse_beta = 1.0 / beta
            target = [beta]
            square = inverse_beta * inverse_beta
            projections = [sums[0] * square]
            length_sq = sums[1] * square
        else:
            projections = [sums[0] * inverse_beta] + sums[1 : column + 1]
            length_sq = sums[column + 1]
        kept = projections[0] * projections[0]
        for value in projections[1:]:
            kept = kept + value * value
        norm_next = jnp.sqrt(length_sq - kept)
        pending = (projections + [norm_next], column)
        if not more:
            break
        inverse = 1.0 / norm_next
        gain = inverse if column else inverse * inverse_beta
        gains = [-(projections[0] * inverse) * inverse_beta] + [
            -(value * inverse) for value in projections[1:]
        ]
        wide = jnp.broadcast_to(gain, (ys, lanes))
        wides = [jnp.broadcast_to(g, (ys, lanes)) for g in gains]

        def combine(x, sums):
            sums = list(sums)
            for k in range(species):
                i = slot(k, x)[0]
                olds = [basis[earlier, i, TOP:high, :] for earlier in range(column + 1)]
                vector = images[column, i, TOP:high, :] * wide
                made = further[i] * wide
                for earlier in range(column + 1):
                    vector = vector + olds[earlier] * wides[earlier]
                    made = made + images[earlier, i, TOP:high, :] * wides[earlier]
                basis[column + 1, i, TOP:high, :] = vector
                images[column + 1, i, TOP:high, :] = made
                for p, left in enumerate(olds + [vector, made]):
                    sums[p] = sums[p] + fold(left * made)
            return tuple(sums)

        share(column + 1, lax.fori_loop(0, xs, combine, (zero,) * (column + 3), unroll=2))
        if wider:
            fresh = finish_halo(r) * gain
            for earlier in range(column + 1):
                fresh = fresh + halos[earlier] * gains[earlier]
            halos.append(fresh)

            def borders(x, carry):
                for k in range(species):
                    i, j = slot(k, x)
                    for side, row in ((0, low), (1, high)):
                        line = yrecv[r, side, pl.ds(j, 1), :] * wide[0:1]
                        for earlier in range(column + 1):
                            line = line + images[earlier, i, row : row + 1, :] * wides[earlier][0:1]
                        images[column + 1, i, row : row + 1, :] = line
                return carry

            lax.fori_loop(0, xs, borders, 0, unroll=2)

    rotate(*pending)
    coeffs = [None] * ITERS
    for column in reversed(range(ITERS)):
        running = target[column]
        for further in range(column + 1, ITERS):
            running = running - triangle[further][column] * coeffs[further]
        coeffs[column] = running * triangle[column][column]
    coeffs[0] = coeffs[0] * inverse_beta
    wides = [jnp.broadcast_to(c, (ys, lanes)) for c in coeffs]

    def finish(x, carry):
        for k in range(species):
            i = slot(k, x)[0]
            total = basis[0, i, TOP:high, :] * wides[0]
            for column in range(1, ITERS):
                total = total + basis[column, i, TOP:high, :] * wides[column]
            out_ref[0, k, x] = total
        return carry

    lax.fori_loop(0, xs, finish, 0, unroll=2)

    for r in range(halo_rounds):
        for inside, _, copy in halo_copies(r):
            @pl.when(inside)
            def _():
                copy.wait_send()
    for column in range(ITERS):
        others = drecv.at[column, pl.ds(0, count - 1)]
        pltpu.make_async_copy(others, others, dsend_sem.at[column]).wait()


def shards(ny, nz, state, member_set, courant, diffusion, reaction, quadratic):
    _, species, xs, ys, lanes = state.shape
    blocks, tall = species * (xs + 2), TOP + ys + 8
    rounds, count = ITERS + 1, ny * nz
    f32 = jnp.float32
    anywhere = pl.BlockSpec(memory_space=pl.ANY)
    tables = (courant.T, diffusion.T, jnp.transpose(reaction, (1, 2, 0)), quadratic.T)
    return pl.pallas_call(
        functools.partial(kernel, ny, nz),
        out_shape=pltpu.VMEM(state.shape, f32),
        in_specs=[anywhere, pl.BlockSpec(memory_space=pltpu.SMEM)] + [anywhere] * len(tables),
        out_specs=pl.BlockSpec(memory_space=pltpu.VMEM),
        scratch_shapes=[pltpu.SMEM(table.shape, table.dtype) for table in tables] + [
            pltpu.SemaphoreType.DMA((len(tables),)),
            pltpu.VMEM((species, xs, ys, lanes), f32),
            pltpu.VMEM((blocks, tall, lanes), f32),
            pltpu.VMEM((blocks, ys, lanes), f32),
            pltpu.VMEM((ITERS, blocks, tall, lanes), f32),
            pltpu.VMEM((ITERS, blocks, tall, lanes), f32),
            pltpu.VMEM((rounds, 2, species * xs, lanes), f32),
            pltpu.VMEM((rounds, 2, species * xs, lanes), f32),
            pltpu.VMEM((rounds, ys, lanes), f32),
            pltpu.VMEM((rounds, 2, ys, lanes), f32),
            pltpu.VMEM((ITERS, 1, lanes), f32),
            pltpu.VMEM((ITERS, count, 1, lanes), f32),
            pltpu.SemaphoreType.DMA((rounds, 2)),
            pltpu.SemaphoreType.DMA((rounds, 2)),
            pltpu.SemaphoreType.DMA((rounds, 2)),
            pltpu.SemaphoreType.DMA((rounds, 2)),
            pltpu.SemaphoreType.DMA((ITERS,)),
            pltpu.SemaphoreType.DMA((ITERS,)),
            pltpu.SemaphoreType.DMA((4 if xs % 8 == 0 else 1,)),
        ],
        compiler_params=pltpu.CompilerParams(collective_id=0, has_side_effects=True),
    )(state, member_set, *tables)


def solution(mesh):
    return jax.shard_map(
        functools.partial(shards, mesh.shape["gy"], mesh.shape["gz"]),
        mesh=mesh,
        in_specs=(P("ens", None, None, "gy", "gz"), P("ens"), P(), P(), P(), P()),
        out_specs=P("ens", None, None, "gy", "gz"),
        check_vma=False,
    )
```
